32 devices in a mesh: frame: 8 (over z, y), row: 4 (over x, core).
Axes of the slice: x: 2, y: 2, z: 4, core: 2. Of those that a mesh axis runs over, the one named last changes fastest.
Arguments:
- features: bfloat16 [16, 64, 64, 640], P('frame', 'row'), may hold values from -6 to 6
- time_weight: bfloat16 [3, 640, 640], replicated, may hold values from -0.125 to 0.125
- time_bias: float32 [640], replicated, may hold values from -3 to 3
- down_weight: bfloat16 [3, 3, 640, 1280], P(None, None, None, 'frame'), may hold values from -0.078125 to 0.078125
- down_bias: float32 [1280], replicated, may hold values from -3 to 3
- norm_gain: float32 [1280], replicated, may hold values from 0.1 to 1.9
- w_query: bfloat16 [1280, 1280], replicated, may hold values from -4 to 4
- w_key: bfloat16 [1280, 1280], replicated, may hold values from -4 to 4
- w_value: bfloat16 [1280, 1280], replicated, may hold values from -0.15625 to 0.15625
- w_out: bfloat16 [1280, 1280], replicated, may hold values from -0.15625 to 0.15625
- out_bias: float32 [1280], replicated, may hold values from -3 to 3
Outputs:
- result: bfloat16 [16, 32, 32, 1280], P('frame', 'row')
The draws below stay inside these ranges and needn't reach their ends.
All inputs are finite; a program needn't handle non-finite values.
Results may differ from the reference program's by a relative error of at most 0.0085.
Values may be sent and summed in bfloat16 or wider, within the bound.
No kernel may reach another device: no remote copies, remote signals or barrier semaphores. Data moves between devices by JAX's collectives and lax.ppermute only.
A program may use at most 192 MiB of HBM per device.

```python
import jax
import jax.numpy as jnp
from jax import lax

C1 = 640
C2 = 1280
HEADS = 16
COLS = 64
FRAMES = 16
ROWS = 64


def paired_normals(key):
    first = jnp.clip(jax.random.normal(jax.random.fold_in(key, 11), (C2, C2), jnp.float32), -6.0, 6.0)
    second = jnp.clip(jax.random.normal(jax.random.fold_in(key, 12), (C2, C2), jnp.float32), -6.0, 6.0)
    return (first, second)


def draw_w_query(key, part):
    first, second = paired_normals(key)
    return (first / C2 ** 0.5).astype(jnp.bfloat16)


def draw_w_key(key, part):
    first, second = paired_normals(key)
    return (second / C2 ** 0.5).astype(jnp.bfloat16)


def shard_levels(key, dims, cuts, smallest, largest):
    gain = 1.0
    for position, blocks in cuts:
        heights = jax.random.uniform(jax.random.fold_in(jax.random.fold_in(key, 6), position), (blocks,), jnp.float32, smallest / len(cuts), largest / len(cuts))
        gain = gain * jnp.repeat(jnp.exp(heights), dims[position] // blocks).reshape((-1,) + (1,) * (len(dims) - 1 - position))
    return gain


def noise(key, extent, scale, bound, split=(), held_as=jnp.bfloat16):
    entries = jax.random.normal(key, extent, jnp.float32) * scale
    if len(split) > 0:
        entries = shard_levels(key, extent, split, -0.22, 0.18) * entries
    return jnp.clip(entries, min=-bound, max=bound).astype(held_as)


def setup_inputs(seed: int = 0) -> dict:
    streams_of = jax.random.split(jax.random.key(seed), 12)
    features = noise(streams_of[0], (FRAMES, ROWS, COLS, C1), 1.0, 6.0, ((0, 8), (1, 4)))
    time_weight = noise(streams_of[1], (3, C1, C1), (3 * C1) ** -0.5, 0.125)
    time_bias = noise(streams_of[2], (C1,), 0.5, 3.0, (), jnp.float32)
    down_weight = noise(streams_of[3], (3, 3, C1, C2), (9 * C1) ** -0.5, 0.078125, ((3, 8),))
    down_bias = noise(streams_of[4], (C2,), 0.5, 3.0, (), jnp.float32)
    norm_gain = jnp.clip(1.0 + 0.18 * jax.random.normal(streams_of[5], (C2,), jnp.float32), 0.1, 1.9)
    w_query = draw_w_query(jax.random.fold_in(streams_of[11], 71), 0)
    w_key = draw_w_key(jax.random.fold_in(streams_of[11], 71), 0)
    w_value = noise(streams_of[8], (C2, C2), C2 ** -0.5, 0.15625)
    w_out = noise(streams_of[9], (C2, C2), C2 ** -0.5, 0.15625)
    out_bias = noise(streams_of[10], (C2,), 0.5, 3.0, (), jnp.float32)
    return dict(features=features, time_weight=time_weight, time_bias=time_bias, down_weight=down_weight, down_bias=down_bias, norm_gain=norm_gain, w_query=w_query, w_key=w_key, w_value=w_value, w_out=w_out, out_bias=out_bias)


def layer_norm(tokens, norm_gain):
    values = tokens.astype(jnp.float32)
    middle_tap = values - lax.optimization_barrier(jnp.mean(values, axis=-1, keepdims=True))
    spread = lax.optimization_barrier(jnp.mean(middle_tap * middle_tap, axis=-1, keepdims=True))
    return (middle_tap * lax.rsqrt(spread + 1e-05) * norm_gain).astype(jnp.bfloat16)

def project(normed, weight):
    return jnp.einsum('fnc,cd->fnd', normed.astype(jnp.float32), weight.astype(jnp.float32)).astype(jnp.bfloat16)

def attend_frames(query_rows, key_rows, value_rows, heads):
    frames, pixels, channels = query_rows.shape
    head_width = channels // heads
    query_heads = query_rows.reshape(frames, pixels, heads, head_width).astype(jnp.float32)
    key_heads = key_rows.reshape(frames, pixels, heads, head_width).astype(jnp.float32)
    value_heads = value_rows.reshape(frames, pixels, heads, head_width).astype(jnp.float32)
    scores = jnp.einsum('fnhd,gnhd->nhfg', query_heads, key_heads) * head_width ** (-0.5)
    weights = jax.nn.softmax(scores, axis=-1).astype(jnp.bfloat16)
    attended = jnp.einsum('nhfg,gnhd->fnhd', weights.astype(jnp.float32), value_heads)
    return attended.astype(jnp.bfloat16).reshape(frames, pixels, channels)

def reference(features, time_weight, time_bias, down_weight, down_bias, norm_gain, w_query, w_key, w_value, w_out, out_bias):
    padded_input = jnp.pad(features, ((1, 1), (0, 0), (0, 0), (0, 0)))
    time_flat = time_weight.reshape(3 * C1, C1)

    def temporal(frame_position):
        window = lax.dynamic_slice_in_dim(padded_input, frame_position, 3, 0)
        stacked = jnp.moveaxis(window, 0, 2).reshape(ROWS * COLS, 3 * C1)
        output = jnp.dot(stacked, time_flat, preferred_element_type=jnp.float32)
        centre = lax.dynamic_index_in_dim(features, frame_position, 0, keepdims=False).reshape(ROWS * COLS, C1)
        summed = centre.astype(jnp.float32) + output + time_bias
        return summed.astype(jnp.bfloat16).reshape(ROWS, COLS, C1)
    hidden_state = lax.map(temporal, jnp.arange(FRAMES, dtype=jnp.int32))
    down_flat = down_weight.reshape(9 * C1, C2)
    half_rows = ROWS // 2
    half_cols = COLS // 2

    def reduce_resolution(single_frame):
        framed = jnp.pad(single_frame, ((1, 1), (1, 1), (0, 0)))
        tap_list = [framed[row_tap:row_tap + 2 * half_rows:2, col_tap:col_tap + 2 * half_cols:2] for row_tap in range(3) for col_tap in range(3)]
        stacked = jnp.concatenate(tap_list, axis=-1).reshape(half_rows * half_cols, 9 * C1)
        output = jnp.dot(stacked, down_flat, preferred_element_type=jnp.float32) + down_bias
        return output.astype(jnp.bfloat16).reshape(half_rows, half_cols, C2)
    coarse_grid = lax.map(reduce_resolution, hidden_state)

    def row_block(tokens):
        normed = layer_norm(tokens, norm_gain)
        attended = attend_frames(project(normed, w_query), project(normed, w_key), project(normed, w_value), HEADS)
        output = jnp.einsum('fnc,cd->fnd', attended.astype(jnp.float32), w_out.astype(jnp.float32))
        return (tokens.astype(jnp.float32) + output + out_bias).astype(jnp.bfloat16)
    result = lax.map(row_block, jnp.moveaxis(coarse_grid, 1, 0))
    return jnp.moveaxis(result, 0, 1)
```

```python
import functools

import jax
import jax.numpy as jnp
from jax import lax
from jax.experimental import pallas as pl
from jax.experimental.pallas import tpu as pltpu
from jax.sharding import PartitionSpec as P

HEADS = 16
LANES = 128
MASKED = -3.0e38


def passed_along(value, axis, steps):
    count = lax.axis_size(axis)
    leading, last = (max(0, -steps), min(count, count - steps))
    return lax.ppermute(value, axis, [(source, source + steps) for source in range(leading, last)])


def weight_part_kernel(part, index_ref, weight_ref, out_ref):
    columns = weight_ref.shape[1]
    rows = lax.broadcasted_iota(jnp.int32, (part, columns), 0) + index_ref[0] * part
    chosen = rows == lax.broadcasted_iota(jnp.int32, (part, columns), 1)
    out_ref[...] = lax.dot_general(
        chosen.astype(jnp.bfloat16),
        weight_ref[...],
        (((1,), (1,)), ((), ())),
        preferred_element_type=jnp.float32,
    ).astype(jnp.bfloat16)


def weight_part(local_columns, parts, index):
    depth, columns = local_columns.shape
    part = columns // parts
    step = depth // 3
    return pl.pallas_call(
        functools.partial(weight_part_kernel, part),
        out_shape=jax.ShapeDtypeStruct((part, depth), jnp.bfloat16),
        grid=(3,),
        in_specs=[
            pl.BlockSpec(memory_space=pltpu.SMEM),
            pl.BlockSpec((step, columns), lambda k: (k, 0)),
        ],
        out_specs=pl.BlockSpec((part, step), lambda k: (0, k)),
        cost_estimate=pl.CostEstimate(
            flops=2 * part * columns * depth, bytes_accessed=2 * depth * (columns + part), transcendentals=0
        ),
    )(index.reshape(1), local_columns)


def temporal_kernel(before_ref, centre_ref, after_ref, weight_ref, bias_ref, out_ref, held):
    rows, columns, channels = centre_ref.shape[1:]
    count = rows * columns
    centre = centre_ref[...].reshape(count, channels)
    total = centre.astype(jnp.float32) + bias_ref[...]
    for tap, value in enumerate((before_ref[...], centre_ref[...], after_ref[...])):
        total = total + jnp.dot(
            value.reshape(count, channels), weight_ref[tap], preferred_element_type=jnp.float32
        )
    total = total.astype(jnp.bfloat16).astype(jnp.float32)
    half = columns // 2
    first = lax.broadcasted_iota(jnp.int32, (rows * half, LANES), 0) % half == 0
    for block in range(channels // LANES):
        low = block * LANES
        held[block, 8:, :] = total[:, low : low + LANES]
        moved = held[block, pl.ds(7, rows * half, stride=2), :]
        even = held[block, pl.ds(8, rows * half, stride=2), :]
        odd = held[block, pl.ds(9, rows * half, stride=2), :]
        moved = jnp.where(first, 0.0, moved)
        for place, plane in enumerate((moved, even, odd)):
            start = place * channels + low
            out_ref[:, 0, :, start : start + LANES] = plane.astype(jnp.bfloat16).reshape(rows, half, LANES)


def temporal(before, centre, after, time_weight, time_bias, rows_step):
    frames, rows, columns, channels = centre.shape
    block = (1, rows_step, columns, channels)
    half = columns // 2
    return pl.pallas_call(
        temporal_kernel,
        out_shape=jax.ShapeDtypeStruct((rows, frames, half, 3 * channels), jnp.bfloat16),
        grid=(frames, rows // rows_step),
        in_specs=[
            pl.BlockSpec(block, lambda f, r: (f, r, 0, 0)),
            pl.BlockSpec(block, lambda f, r: (f, r, 0, 0)),
            pl.BlockSpec(block, lambda f, r: (f, r, 0, 0)),
            pl.BlockSpec(time_weight.shape, lambda f, r: (0, 0, 0)),
            pl.BlockSpec((1, channels), lambda f, r: (0, 0)),
        ],
        out_specs=pl.BlockSpec((rows_step, 1, half, 3 * channels), lambda f, r: (r, f, 0, 0)),
        scratch_shapes=[
            pltpu.VMEM((channels // LANES, 8 + rows_step * columns, LANES), jnp.float32)
        ],
        cost_estimate=pl.CostEstimate(
            flops=6 * frames * rows * columns * channels * channels,
            bytes_accessed=9 * frames * rows * columns * channels,
            transcendentals=0,
        ),
    )(before, centre, after, time_weight, time_bias.reshape(1, channels))


def strided_kernel(planes_ref, upper_ref, weight_ref, bias_ref, out_ref, total):
    row_tap = pl.program_id(1)
    half_rows, _, frames, half_cols, width = planes_ref.shape
    count = half_rows * frames * half_cols

    def product(values):
        return lax.dot_general(
            values.reshape(count, width),
            weight_ref[...],
            (((1,), (1,)), ((), ())),
            preferred_element_type=jnp.float32,
        )

    @pl.when(row_tap == 0)
    def _():
        values = jnp.concatenate([upper_ref[...], planes_ref[: half_rows - 1, 1]], axis=0)
        total[...] = product(values) + bias_ref[...]

    @pl.when(row_tap == 1)
    def _():
        total[...] += product(planes_ref[:, 0])

    @pl.when(row_tap == 2)
    def _():
        done = total[...] + product(planes_ref[:, 1])
        out_ref[...] = done.astype(jnp.bfloat16).reshape(out_ref.shape)


def strided(planes, upper, weight, bias, step):
    rows, frames, half_cols, width = planes.shape
    channels = weight.shape[0]
    half_rows = rows // 2
    count = half_rows * frames * half_cols
    return pl.pallas_call(
        strided_kernel,
        out_shape=jax.ShapeDtypeStruct((half_rows, frames, half_cols, channels), jnp.bfloat16),
        grid=(channels // step, 3),
        in_specs=[
            pl.BlockSpec((half_rows, 2, frames, half_cols, width), lambda n, a: (0, 0, 0, 0, 0)),
            pl.BlockSpec((1, frames, half_cols, width), lambda n, a: (0, 0, 0, 0)),
            pl.BlockSpec((step, width), lambda n, a: (n, a)),
            pl.BlockSpec((1, step), lambda n, a: (0, n)),
        ],
        out_specs=pl.BlockSpec((half_rows, frames, half_cols, step), lambda n, a: (0, 0, 0, n)),
        scratch_shapes=[pltpu.VMEM((count, step), jnp.float32)],
        cost_estimate=pl.CostEstimate(
            flops=6 * count * width * channels,
            bytes_accessed=2 * (planes.size + weight.size + count * channels),
            transcendentals=0,
        ),
    )(planes.reshape(half_rows, 2, frames, half_cols, width), upper, weight, bias.reshape(1, channels))


def attention_kernel(
    tokens_ref, gain_ref, bias_ref, wq_hbm, wk_hbm, wv_hbm, wo_hbm, out_ref,
    wq, wk, wv, wo, normed, query, key, value, sems,
):
    copies = []
    for place, (source, target) in enumerate(((wq_hbm, wq), (wk_hbm, wk), (wv_hbm, wv), (wo_hbm, wo))):
        copies.append(pltpu.make_async_copy(source, target, sems.at[place]))
        copies[-1].start()
    frames, pixels, width = tokens_ref.shape
    groups = pixels // 8
    rows = frames * 8
    head_width = width // HEADS
    scale = head_width ** (-0.5)
    for group in range(groups):
        tokens = tokens_ref[:, group * 8 : group * 8 + 8, :].astype(jnp.float32).reshape(rows, width)
        centred = tokens - jnp.mean(tokens, axis=-1, keepdims=True)
        spread = jnp.mean(centred * centred, axis=-1, keepdims=True)
        result = centred * lax.rsqrt(spread + 1e-05) * gain_ref[...]
        normed[group * rows : (group + 1) * rows, :] = result.astype(jnp.bfloat16)
    step = 256
    for place, (weight, target) in enumerate(((wq, query), (wk, key), (wv, value))):
        copies[place].wait()

        @pl.loop(0, width // step)
        def _(n):
            part = pl.ds(pl.multiple_of(n * step, step), step)
            target[:, part] = jnp.dot(
                normed[...], weight[:, part], preferred_element_type=jnp.float32
            ).astype(jnp.bfloat16)

    same = (
        lax.broadcasted_iota(jnp.int32, (rows, rows), 0) % 8
        == lax.broadcasted_iota(jnp.int32, (rows, rows), 1) % 8
    )

    @pl.loop(0, groups)
    def _(group):
        here = pl.ds(pl.multiple_of(group * rows, rows), rows)
        sums = [None] * (width // LANES)
        for head in range(HEADS):
            low = head * head_width // LANES
            high = ((head + 1) * head_width - 1) // LANES + 1
            window = slice(low * LANES, high * LANES)
            lane = lax.broadcasted_iota(jnp.int32, (rows, (high - low) * LANES), 1) + low * LANES
            mine = (lane >= head * head_width) & (lane < (head + 1) * head_width)
            zeros = jnp.zeros((rows, (high - low) * LANES), jnp.bfloat16)
            queries = jnp.where(mine, query[here, window], zeros)
            scores = lax.dot_general(
                queries, key[here, window], (((1,), (1,)), ((), ())), preferred_element_type=jnp.float32
            )
            scores = jnp.where(same, scores * scale, MASKED)
            powers = jnp.exp(scores - jnp.max(scores, axis=-1, keepdims=True))
            weights = powers * (1.0 / jnp.sum(powers, axis=-1, keepdims=True))
            values = jnp.where(mine, value[here, window], zeros)
            part = jnp.dot(weights.astype(jnp.bfloat16), values, preferred_element_type=jnp.float32)
            for block in range(low, high):
                piece = part[:, (block - low) * LANES : (block - low + 1) * LANES]
                sums[block] = piece if sums[block] is None else sums[block] + piece
        for block, total in enumerate(sums):
            normed[here, block * LANES : (block + 1) * LANES] = total.astype(jnp.bfloat16)

    copies[3].wait()

    @pl.loop(0, width // step)
    def _(n):
        part = pl.ds(pl.multiple_of(n * step, step), step)
        output = jnp.dot(normed[...], wo[:, part], preferred_element_type=jnp.float32)
        output = output + bias_ref[:, part]
        for group in range(groups):
            tokens = tokens_ref[:, group * 8 : group * 8 + 8, part].astype(jnp.float32)
            piece = output[group * rows : (group + 1) * rows].reshape(frames, 8, step) + tokens
            out_ref[:, group * 8 : group * 8 + 8, part] = piece.astype(jnp.bfloat16)


def attention(tokens, norm_gain, out_bias, w_query, w_key, w_value, w_out):
    frames, pixels, width = tokens.shape
    count = frames * pixels
    weight = pltpu.VMEM((width, width), jnp.bfloat16)
    rows = pltpu.VMEM((count, width), jnp.bfloat16)
    anywhere = pl.BlockSpec(memory_space=pl.ANY)
    inside = pl.BlockSpec(memory_space=pltpu.VMEM)
    return pl.pallas_call(
        attention_kernel,
        out_shape=jax.ShapeDtypeStruct(tokens.shape, jnp.bfloat16),
        in_specs=[inside, inside, inside, anywhere, anywhere, anywhere, anywhere],
        out_specs=inside,
        scratch_shapes=[weight] * 4 + [rows] * 4 + [pltpu.SemaphoreType.DMA((4,))],
        cost_estimate=pl.CostEstimate(
            flops=8 * count * width * width,
            bytes_accessed=8 * width * width + 4 * count * width,
            transcendentals=count * HEADS * frames * 8,
        ),
    )(
        tokens, norm_gain.reshape(1, width), out_bias.reshape(1, width), w_query, w_key, w_value, w_out
    )


def on_device(
    features,
    time_weight,
    time_bias,
    down_weight,
    down_bias,
    norm_gain,
    w_query,
    w_key,
    w_value,
    w_out,
    out_bias,
):
    frames_here, rows_here, columns, channels = features.shape
    groups = lax.axis_size("frame")
    row_devices = lax.axis_size("row")
    local_columns = down_weight.reshape(9 * channels, down_weight.shape[3])
    part = weight_part(local_columns, row_devices, lax.axis_index("row"))
    weight = lax.all_gather(part, ("frame", "row"), axis=0, tiled=True)
    model_width = weight.shape[0]

    low = passed_along(features[-1:], "frame", 1)
    high = passed_along(features[:1], "frame", -1)
    before = jnp.concatenate([low, features[:-1]], axis=0)
    after = jnp.concatenate([features[1:], high], axis=0)
    planes = temporal(before, features, after, time_weight, time_bias, rows_here // 2)
    upper = passed_along(planes[-1:], "row", 1)
    coarse = strided(planes, upper, weight, down_bias, 256)

    half_rows, half_cols = rows_here // 2, columns // 2
    pixels_here = half_rows * half_cols // groups
    tokens = coarse
    if groups != half_rows:
        tokens = tokens.transpose(1, 0, 2, 3).reshape(frames_here, groups, pixels_here, model_width)
        tokens = tokens.transpose(1, 0, 2, 3)
    moved = lax.all_to_all(tokens, "frame", split_axis=0, concat_axis=0, tiled=True)
    moved = moved.reshape(groups * frames_here, pixels_here, model_width)
    result = attention(moved, norm_gain, out_bias, w_query, w_key, w_value, w_out)
    result = result.reshape(groups, frames_here, pixels_here, model_width)
    returned = lax.all_to_all(result, "frame", split_axis=0, concat_axis=0, tiled=True)
    returned = returned.transpose(1, 0, 2, 3)
    return returned.reshape(frames_here, half_rows, half_cols, model_width)


def solution(mesh):
    return jax.shard_map(
        on_device,
        mesh=mesh,
        in_specs=(
            P("frame", "row", None, None),
            P(),
            P(),
            P(None, None, None, "frame"),
            P(),
            P(),
            P(),
            P(),
            P(),
            P(),
            P(),
        ),
        out_specs=P("frame", "row", None, None),
        check_vma=False,
    )
```

```python
import functools

import jax
import jax.numpy as jnp
from jax import lax
from jax.experimental import pallas as pl
from jax.experimental.pallas import tpu as pltpu
from jax.sharding import PartitionSpec as P


HEADS = 16
LANES = 128
MASKED = -3.0e38


def passed_along(value, axis, steps):
    count = lax.axis_size(axis)
    leading, last = (max(0, -steps), min(count, count - steps))
    return lax.ppermute(value, axis, [(source, source + steps) for source in range(leading, last)])


def temporal_kernel(*refs):
    *frame_refs, weight_ref, bias_ref, out_ref, held = refs
    rows, columns, channels = frame_refs[0].shape[1:]
    count = rows * columns
    values = [ref[...].reshape(count, channels) for ref in frame_refs]
    half = columns // 2
    first = lax.broadcasted_iota(jnp.int32, (rows * half, LANES), 0) % half == 0
    for place in range(len(values) - 2):
        window = jnp.concatenate(values[place : place + 3], axis=1)
        total = jnp.dot(window, weight_ref[...], preferred_element_type=jnp.float32)
        total = total + (values[place + 1].astype(jnp.float32) + bias_ref[...])
        total = total.astype(jnp.bfloat16).astype(jnp.float32)
        for block in range(channels // LANES):
            low = block * LANES
            held[block, 8:, :] = total[:, low : low + LANES]
            moved = held[block, pl.ds(7, rows * half, stride=2), :]
            even = held[block, pl.ds(8, rows * half, stride=2), :]
            odd = held[block, pl.ds(9, rows * half, stride=2), :]
            moved = jnp.where(first, 0.0, moved)
            for tap, plane in enumerate((moved, even, odd)):
                start = tap * channels + low
                out_ref[:, place, :, start : start + LANES] = plane.astype(jnp.bfloat16).reshape(
                    rows, half, LANES
                )


def temporal(sequence, time_weight, time_bias, start, rows, step):
    _, _, columns, channels = sequence[0].shape
    frames = len(sequence) - 2
    half = columns // 2
    return pl.pallas_call(
        temporal_kernel,
        out_shape=jax.ShapeDtypeStruct((rows, frames, half, 3 * channels), jnp.bfloat16),
        grid=(rows // step,),
        in_specs=[pl.BlockSpec((1, step, columns, channels), lambda r: (0, r + start // step, 0, 0))]
        * len(sequence)
        + [
            pl.BlockSpec((3 * channels, channels), lambda r: (0, 0)),
            pl.BlockSpec((1, channels), lambda r: (0, 0)),
        ],
        out_specs=pl.BlockSpec((step, frames, half, 3 * channels), lambda r: (r, 0, 0, 0)),
        scratch_shapes=[pltpu.VMEM((channels // LANES, 8 + step * columns, LANES), jnp.float32)],
        cost_estimate=pl.CostEstimate(
            flops=6 * frames * rows * columns * channels * channels,
            bytes_accessed=2 * (5 * frames + 2) * rows * columns * channels,
            transcendentals=0,
        ),
    )(*sequence, time_weight.reshape(3 * channels, channels), time_bias.reshape(1, channels))


def strided_kernel(spans, where_ref, planes_ref, upper_ref, bias_ref, *refs):
    pieces, (out_ref, weight, total, sems) = refs[: len(spans)], refs[len(spans) :]
    step = pl.program_id(0)
    half_rows, _, frames, half_cols, width = planes_ref.shape
    count = half_rows * frames * half_cols
    channels = width // 3
    _, units, unit, _ = weight.shape

    def copies():
        for place, (piece, (taps, run)) in enumerate(zip(pieces, spans)):
            target = weight.at[pl.ds(where_ref[place, 0], taps), pl.ds(where_ref[place, 1], run)]
            yield pltpu.make_async_copy(piece, target, sems.at[place])

    def product(values, tap):
        result = None
        for part in range(3):
            term = lax.dot_general(
                values[..., part * channels : (part + 1) * channels].reshape(count, channels),
                weight[3 * tap + part].reshape(units * unit, channels),
                (((1,), (1,)), ((), ())),
                preferred_element_type=jnp.float32,
            )
            result = term if result is None else result + term
        return result

    @pl.when(step == 0)
    def _():
        for copy in copies():
            copy.start()
        for copy in copies():
            copy.wait()
        values = jnp.concatenate([upper_ref[...], planes_ref[: half_rows - 1, 1]], axis=0)
        total[...] = product(values, 0) + bias_ref[...]

    @pl.when(step == 1)
    def _():
        total[...] += product(planes_ref[:, 0], 1)

    @pl.when(step == 2)
    def _():
        done = total[...] + product(planes_ref[:, 1], 2)
        out_ref[...] = done.astype(jnp.bfloat16).reshape(out_ref.shape)


def strided(planes, upper, pieces, where, bias):
    rows, frames, half_cols, width = planes.shape
    outputs = bias.shape[0]
    half_rows = rows // 2
    count = half_rows * frames * half_cols
    unit = pieces[0].shape[2]
    channels = width // 3
    anywhere = pl.BlockSpec(memory_space=pl.ANY)
    return pl.pallas_call(
        functools.partial(strided_kernel, tuple(piece.shape[:2] for piece in pieces)),
        out_shape=jax.ShapeDtypeStruct((half_rows, frames, half_cols, outputs), jnp.bfloat16),
        grid=(3,),
        in_specs=[
            pl.BlockSpec(memory_space=pltpu.SMEM),
            pl.BlockSpec((half_rows, 2, frames, half_cols, width), lambda a: (0, 0, 0, 0, 0)),
            pl.BlockSpec((1, frames, half_cols, width), lambda a: (0, 0, 0, 0)),
            pl.BlockSpec((1, outputs), lambda a: (0, 0)),
        ]
        + [anywhere] * len(pieces),
        out_specs=pl.BlockSpec((half_rows, frames, half_cols, outputs), lambda a: (0, 0, 0, 0)),
        scratch_shapes=[
            pltpu.VMEM((9, outputs // unit, unit, channels), jnp.bfloat16),
            pltpu.VMEM((count, outputs), jnp.float32),
            pltpu.SemaphoreType.DMA((len(pieces),)),
        ],
        cost_estimate=pl.CostEstimate(
            flops=6 * count * width * outputs,
            bytes_accessed=2 * (planes.size + 3 * width * outputs + count * outputs),
            transcendentals=0,
        ),
    )(
        where,
        planes.reshape(half_rows, 2, frames, half_cols, width),
        upper,
        bias.reshape(1, outputs),
        *pieces,
    )


def attention_kernel(
    tokens_ref, gain_ref, bias_ref, wq_hbm, wk_hbm, wv_hbm, wo_hbm, out_ref,
    wq, wk, wv, wo, held, normed, query, key, value, sems,
):
    copies = []
    for place, (source, target) in enumerate(((wq_hbm, wq), (wk_hbm, wk), (wv_hbm, wv), (wo_hbm, wo))):
        copies.append(pltpu.make_async_copy(source, target, sems.at[place]))
        copies[-1].start()
    frames, pixels, width = out_ref.shape
    groups = pixels // 8
    rows = frames * 8
    sources, span, _, half_width = tokens_ref.shape
    share = half_width // (sources // 2)
    head_width = width // HEADS
    scale = head_width ** (-0.5)
    for group in range(groups):
        here = slice(group * 8, group * 8 + 8)
        low = [tokens_ref[2 * line, :, here, :] for line in range(sources // 2)]
        high = [tokens_ref[2 * line + 1, span - 1 - at, here, :] for line in range(sources // 2) for at in range(span)]
        low = jnp.concatenate([value.astype(jnp.float32).reshape(span * 8, half_width) for value in low], axis=0)
        high = jnp.concatenate([value.astype(jnp.float32) for value in high], axis=0)
        parts = []
        for line in range(sources // 2):
            parts += [low[:, line * share : (line + 1) * share], high[:, line * share : (line + 1) * share]]
        tokens = jnp.concatenate(parts, axis=1)
        held[group * rows : (group + 1) * rows, :] = tokens.astype(jnp.bfloat16)
        centred = tokens - jnp.mean(tokens, axis=-1, keepdims=True)
        spread = jnp.mean(centred * centred, axis=-1, keepdims=True)
        result = centred * lax.rsqrt(spread + 1e-05) * gain_ref[...]
        normed[group * rows : (group + 1) * rows, :] = result.astype(jnp.bfloat16)
    step = 256
    for place, (weight, target) in enumerate(((wq, query), (wk, key), (wv, value))):
        copies[place].wait()

        @pl.loop(0, width // step)
        def _(n):
            part = pl.ds(pl.multiple_of(n * step, step), step)
            target[:, part] = jnp.dot(
                normed[...], weight[:, part], preferred_element_type=jnp.float32
            ).astype(jnp.bfloat16)

    same = (
        lax.broadcasted_iota(jnp.int32, (rows, rows), 0) % 8
        == lax.broadcasted_iota(jnp.int32, (rows, rows), 1) % 8
    )

    @pl.loop(0, groups)
    def _(group):
        here = pl.ds(pl.multiple_of(group * rows, rows), rows)
        sums = [None] * (width // LANES)
        for head in range(HEADS):
            low = head * head_width // LANES
            high = ((head + 1) * head_width - 1) // LANES + 1
            window = slice(low * LANES, high * LANES)
            lane = lax.broadcasted_iota(jnp.int32, (rows, (high - low) * LANES), 1) + low * LANES
            mine = (lane >= head * head_width) & (lane < (head + 1) * head_width)
            zeros = jnp.zeros((rows, (high - low) * LANES), jnp.bfloat16)
            queries = jnp.where(mine, query[here, window], zeros)
            scores = lax.dot_general(
                queries, key[here, window], (((1,), (1,)), ((), ())), preferred_element_type=jnp.float32
            )
            scores = jnp.where(same, scores * scale, MASKED)
            powers = jnp.exp(scores - jnp.max(scores, axis=-1, keepdims=True))
            weights = powers * (1.0 / jnp.sum(powers, axis=-1, keepdims=True))
            values = jnp.where(mine, value[here, window], zeros)
            part = jnp.dot(weights.astype(jnp.bfloat16), values, preferred_element_type=jnp.float32)
            for block in range(low, high):
                piece = part[:, (block - low) * LANES : (block - low + 1) * LANES]
                sums[block] = piece if sums[block] is None else sums[block] + piece
        for block, total in enumerate(sums):
            normed[here, block * LANES : (block + 1) * LANES] = total.astype(jnp.bfloat16)

    copies[3].wait()

    @pl.loop(0, width // step)
    def _(n):
        part = pl.ds(pl.multiple_of(n * step, step), step)
        output = jnp.dot(normed[...], wo[:, part], preferred_element_type=jnp.float32)
        output = output + bias_ref[:, part]
        for group in range(groups):
            here = slice(group * rows, (group + 1) * rows)
            piece = (output[here] + held[here, part].astype(jnp.float32)).reshape(frames, 8, step)
            out_ref[:, group * 8 : group * 8 + 8, part] = piece.astype(jnp.bfloat16)


def attention(tokens, norm_gain, out_bias, w_query, w_key, w_value, w_out):
    sources, span, pixels, half_width = tokens.shape
    frames, width = sources * span // 2, 2 * half_width
    count = frames * pixels
    weight = pltpu.VMEM((width, width), jnp.bfloat16)
    rows = pltpu.VMEM((count, width), jnp.bfloat16)
    anywhere = pl.BlockSpec(memory_space=pl.ANY)
    inside = pl.BlockSpec(memory_space=pltpu.VMEM)
    return pl.pallas_call(
        attention_kernel,
        out_shape=jax.ShapeDtypeStruct((frames, pixels, width), jnp.bfloat16),
        in_specs=[inside, inside, inside, anywhere, anywhere, anywhere, anywhere],
        out_specs=inside,
        scratch_shapes=[weight] * 4 + [rows] * 5 + [pltpu.SemaphoreType.DMA((4,))],
        cost_estimate=pl.CostEstimate(
            flops=8 * count * width * width,
            bytes_accessed=8 * width * width + 4 * count * width,
            transcendentals=count * HEADS * frames * 8,
        ),
    )(
        tokens, norm_gain.reshape(1, width), out_bias.reshape(1, width), w_query, w_key, w_value, w_out
    )


def on_device(
    features,
    time_weight,
    time_bias,
    down_weight,
    down_bias,
    norm_gain,
    w_query,
    w_key,
    w_value,
    w_out,
    out_bias,
):
    frames_here, rows_here, columns, channels = features.shape
    groups = lax.axis_size("frame")
    lines = groups // 2
    frame, row = lax.axis_index("frame"), lax.axis_index("row")
    line, side = frame // 2, frame % 2

    everyone = range(groups)
    swapped = [(at, at ^ 1) for at in everyone]
    own = [
        lax.dynamic_slice_in_dim(features, jnp.where(side == 0, at, frames_here - 1 - at), 1, axis=0)
        for at in range(frames_here)
    ]
    other = [lax.ppermute(value, "frame", swapped) for value in own]
    outward = [(at, at + (2 if at % 2 else -2)) for at in everyone]
    inward = [(at, at + (-2 if at % 2 else 2)) for at in everyone]
    inside = lambda pairs: [(source, target) for source, target in pairs if 0 <= target < groups]
    last = lax.ppermute(own[0], "frame", inside(outward))
    first = lax.ppermute(other[0], "frame", inside(inward))
    sequence = [first] + own + other[::-1] + [last]

    pieces, where = strided_weights(down_weight, frame, row, channels)

    taps = jnp.where(side == 0, time_weight, time_weight[::-1])
    final = temporal(sequence, taps, time_bias, rows_here - 1, 1, 1)
    upper = passed_along(final, "row", 1)
    planes = temporal(sequence, taps, time_bias, 0, rows_here, 2)
    shares = down_bias.reshape(lines, 2, down_bias.shape[0] // groups)
    bias = lax.dynamic_index_in_dim(shares, side, axis=1, keepdims=False).reshape(-1)
    coarse = strided(planes, upper, pieces, where, bias)

    half_rows, half_cols = rows_here // 2, columns // 2
    half_width = coarse.shape[-1]
    pixels_here = half_rows * half_cols // groups
    tokens = coarse
    if groups != half_rows:
        tokens = tokens.transpose(1, 0, 2, 3).reshape(2 * frames_here, groups, pixels_here, half_width)
        tokens = tokens.transpose(1, 0, 2, 3)
    moved = lax.all_to_all(tokens, "frame", split_axis=0, concat_axis=0, tiled=True)
    result = attention(moved, norm_gain, out_bias, w_query, w_key, w_value, w_out)
    result = result.reshape(groups, frames_here, pixels_here, 2 * half_width)
    returned = lax.all_to_all(result, "frame", split_axis=0, concat_axis=0, tiled=True)
    returned = returned.transpose(1, 0, 2, 3)
    return returned.reshape(frames_here, half_rows, half_cols, 2 * half_width)


def strided_weights(down_weight, frame, row, channels):
    groups, row_devices = lax.axis_size("frame"), lax.axis_size("row")
    lines = groups // 2
    share = down_weight.shape[3]
    line = frame // 2
    shard = down_weight.transpose(0, 1, 3, 2).reshape(9, share, channels)
    unit = share // 2
    if unit % 16 or lines & (lines - 1) or row_devices % 4:
        members = [[2 * at + side for at in range(lines)] for side in range(2)]
        gathered = lax.all_gather(shard, "frame", axis=1, tiled=True, axis_index_groups=members)
        return [gathered[:, None]], jnp.zeros((1, 2), jnp.int32)
    core, plane = row % 2, row // 2 % 2
    shard = shard.reshape(9, 2, unit, channels)
    pieces, where = [shard], [(0, 2 * line)]
    mine = lax.dynamic_slice(shard, (4 * plane, core, 0, 0), (5, 1, unit, channels))
    rows = range(row_devices)
    for distance in range(1, lines):
        place = 2 * (line ^ distance)
        steps = [(at, (at // 2 ^ distance) * 2 + at % 2) for at in range(groups)]
        near = lax.ppermute(mine, "frame", steps)
        sent = lax.dynamic_slice_in_dim(near, plane, 4, axis=0)
        far = lax.ppermute(sent, "row", [(at, at ^ 2) for at in rows])
        pieces += [near, far]
        where += [(4 * plane, place + core), (5 - 5 * plane, place + core)]
        for value, tap in ((near, 4 * plane), (far, 5 - 5 * plane)):
            pieces.append(lax.ppermute(value, "row", [(at, at ^ 1) for at in rows]))
            where.append((tap, place + 1 - core))
    return pieces, jnp.stack([jnp.stack([jnp.int32(tap), jnp.int32(at)]) for tap, at in where])


def solution(mesh):
    return jax.shard_map(
        on_device,
        mesh=mesh,
        in_specs=(
            P("frame", "row", None, None),
            P(),
            P(),
            P(None, None, None, "frame"),
            P(),
            P(),
            P(),
            P(),
            P(),
            P(),
            P(),
        ),
        out_specs=P("frame", "row", None, None),
        check_vma=False,
    )
```

```python
import functools

import jax
import jax.numpy as jnp
from jax import lax
from jax.experimental import pallas as pl
from jax.experimental.pallas import tpu as pltpu
from jax.sharding import PartitionSpec as P


HEADS = 16
LANES = 128
MASKED = -3.0e38


def passed_along(value, axis, steps):
    count = lax.axis_size(axis)
    leading, last = (max(0, -steps), min(count, count - steps))
    return lax.ppermute(value, axis, [(source, source + steps) for source in range(leading, last)])


def temporal_kernel(*refs):
    *frame_refs, weight_ref, bias_ref, out_ref, held = refs
    rows, columns, channels = frame_refs[0].shape[1:]
    frames = len(frame_refs) - 2
    count = rows * columns
    values = [ref[...].reshape(count, channels) for ref in frame_refs]
    stacked = [jnp.concatenate(values[tap : tap + frames], axis=0) for tap in range(3)]
    total = jnp.dot(jnp.concatenate(stacked, axis=1), weight_ref[...], preferred_element_type=jnp.float32)
    total = total + (stacked[1].astype(jnp.float32) + bias_ref[...])
    total = total.astype(jnp.bfloat16).astype(jnp.float32)
    lanes = channels // LANES
    for block in range(lanes):
        held[block, 8:, :] = total[:, block * LANES : (block + 1) * LANES]
    half = columns // 2
    first = lax.broadcasted_iota(jnp.int32, (rows * half, LANES), 0) % half == 0
    for place in range(frames):
        for block in range(lanes):
            begin = place * count
            moved = held[block, pl.ds(begin + 7, rows * half, stride=2), :]
            even = held[block, pl.ds(begin + 8, rows * half, stride=2), :]
            odd = held[block, pl.ds(begin + 9, rows * half, stride=2), :]
            moved = jnp.where(first, 0.0, moved)
            for tap, plane in enumerate((moved, even, odd)):
                start = tap * channels + block * LANES
                out_ref[:, place, :, start : start + LANES] = plane.astype(jnp.bfloat16).reshape(
                    rows, half, LANES
                )


def temporal(sequence, time_weight, time_bias, start, rows, step):
    _, _, columns, channels = sequence[0].shape
    frames = len(sequence) - 2
    half = columns // 2
    return pl.pallas_call(
        temporal_kernel,
        out_shape=jax.ShapeDtypeStruct((rows, frames, half, 3 * channels), jnp.bfloat16),
        grid=(rows // step,),
        in_specs=[pl.BlockSpec((1, step, columns, channels), lambda r: (0, r + start // step, 0, 0))]
        * len(sequence)
        + [
            pl.BlockSpec((3 * channels, channels), lambda r: (0, 0)),
            pl.BlockSpec((1, channels), lambda r: (0, 0)),
        ],
        out_specs=pl.BlockSpec((step, frames, half, 3 * channels), lambda r: (r, 0, 0, 0)),
        scratch_shapes=[pltpu.VMEM((channels // LANES, 8 + frames * step * columns, LANES), jnp.float32)],
        cost_estimate=pl.CostEstimate(
            flops=6 * frames * rows * columns * channels * channels,
            bytes_accessed=2 * (5 * frames + 2) * rows * columns * channels,
            transcendentals=0,
        ),
    )(*sequence, time_weight.reshape(3 * channels, channels), time_bias.reshape(1, channels))


def strided_kernel(spans, where_ref, planes_ref, upper_ref, bias_ref, *refs):
    pieces, (*out_refs, weight, total, sems) = refs[: len(spans)], refs[len(spans) :]
    step = pl.program_id(0)
    half_rows, _, frames, half_cols, width = planes_ref.shape
    count = half_rows * frames * half_cols
    channels = width // 3
    _, units, unit, _ = weight.shape

    def copies():
        for place, (piece, (taps, run)) in enumerate(zip(pieces, spans)):
            target = weight.at[pl.ds(where_ref[place, 0], taps), pl.ds(where_ref[place, 1], run)]
            yield pltpu.make_async_copy(piece, target, sems.at[place])

    def product(values, tap):
        result = None
        for part in range(3):
            term = lax.dot_general(
                values[..., part * channels : (part + 1) * channels].reshape(count, channels),
                weight[3 * tap + part].reshape(units * unit, channels),
                (((1,), (1,)), ((), ())),
                preferred_element_type=jnp.float32,
            )
            result = term if result is None else result + term
        return result

    @pl.when(step == 0)
    def _():
        for copy in copies():
            copy.start()
        for copy in copies():
            copy.wait()
        values = jnp.concatenate([upper_ref[...], planes_ref[: half_rows - 1, 1]], axis=0)
        total[...] = product(values, 0) + bias_ref[...]

    @pl.when(step == 1)
    def _():
        total[...] += product(planes_ref[:, 0], 1)

    @pl.when(step == 2)
    def _():
        done = total[...] + product(planes_ref[:, 1], 2)
        done = done.reshape(half_rows, frames, half_cols, done.shape[1])
        part = half_cols // len(out_refs)
        for chunk, out_ref in enumerate(out_refs):
            out_ref[...] = done[:, :, chunk * part : (chunk + 1) * part].astype(jnp.bfloat16)


def strided(planes, upper, pieces, where, bias, chunks):
    rows, frames, half_cols, width = planes.shape
    outputs = bias.shape[0]
    half_rows = rows // 2
    count = half_rows * frames * half_cols
    unit = pieces[0].shape[2]
    channels = width // 3
    block = (half_rows, frames, half_cols // chunks, outputs)
    anywhere = pl.BlockSpec(memory_space=pl.ANY)
    return pl.pallas_call(
        functools.partial(strided_kernel, tuple(piece.shape[:2] for piece in pieces)),
        out_shape=[jax.ShapeDtypeStruct(block, jnp.bfloat16)] * chunks,
        grid=(3,),
        in_specs=[
            pl.BlockSpec(memory_space=pltpu.SMEM),
            pl.BlockSpec((half_rows, 2, frames, half_cols, width), lambda a: (0, 0, 0, 0, 0)),
            pl.BlockSpec((1, frames, half_cols, width), lambda a: (0, 0, 0, 0)),
            pl.BlockSpec((1, outputs), lambda a: (0, 0)),
        ]
        + [anywhere] * len(pieces),
        out_specs=[pl.BlockSpec(block, lambda a: (0, 0, 0, 0))] * chunks,
        scratch_shapes=[
            pltpu.VMEM((9, outputs // unit, unit, channels), jnp.bfloat16),
            pltpu.VMEM((count, outputs), jnp.float32),
            pltpu.SemaphoreType.DMA((len(pieces),)),
        ],
        cost_estimate=pl.CostEstimate(
            flops=6 * count * width * outputs,
            bytes_accessed=2 * (planes.size + 3 * width * outputs + count * outputs),
            transcendentals=0,
        ),
    )(
        where,
        planes.reshape(half_rows, 2, frames, half_cols, width),
        upper,
        bias.reshape(1, outputs),
        *pieces,
    )


def attention_kernel(
    tokens_ref, gain_ref, bias_ref, wq_hbm, wk_hbm, wv_hbm, wo_hbm, out_ref,
    wq, wk, wv, wo, held, normed, query, key, value, sems,
):
    copies = []
    for place, (source, target) in enumerate(((wq_hbm, wq), (wk_hbm, wk), (wv_hbm, wv), (wo_hbm, wo))):
        copies.append(pltpu.make_async_copy(source, target, sems.at[place]))
        copies[-1].start()
    frames, pixels, width = out_ref.shape
    groups = pixels // 8
    rows = frames * 8
    sources, span, _, half_width = tokens_ref.shape
    share = half_width // (sources // 2)
    head_width = width // HEADS
    scale = head_width ** (-0.5)
    for group in range(groups):
        here = slice(group * 8, group * 8 + 8)
        low = [tokens_ref[2 * line, :, here, :] for line in range(sources // 2)]
        high = [tokens_ref[2 * line + 1, span - 1 - at, here, :] for line in range(sources // 2) for at in range(span)]
        low = jnp.concatenate([value.astype(jnp.float32).reshape(span * 8, half_width) for value in low], axis=0)
        high = jnp.concatenate([value.astype(jnp.float32) for value in high], axis=0)
        parts = []
        for line in range(sources // 2):
            parts += [low[:, line * share : (line + 1) * share], high[:, line * share : (line + 1) * share]]
        tokens = jnp.concatenate(parts, axis=1)
        held[group * rows : (group + 1) * rows, :] = tokens.astype(jnp.bfloat16)
        centred = tokens - jnp.mean(tokens, axis=-1, keepdims=True)
        spread = jnp.mean(centred * centred, axis=-1, keepdims=True)
        result = centred * lax.rsqrt(spread + 1e-05) * gain_ref[...]
        normed[group * rows : (group + 1) * rows, :] = result.astype(jnp.bfloat16)
    step = 256
    for place, (weight, target) in enumerate(((wq, query), (wk, key), (wv, value))):
        copies[place].wait()

        @pl.loop(0, width // step)
        def _(n):
            part = pl.ds(pl.multiple_of(n * step, step), step)
            target[:, part] = jnp.dot(
                normed[...], weight[:, part], preferred_element_type=jnp.float32
            ).astype(jnp.bfloat16)

    same = (
        lax.broadcasted_iota(jnp.int32, (rows, rows), 0) % 8
        == lax.broadcasted_iota(jnp.int32, (rows, rows), 1) % 8
    )

    @pl.loop(0, groups)
    def _(group):
        here = pl.ds(pl.multiple_of(group * rows, rows), rows)
        sums = [None] * (width // LANES)
        for head in range(HEADS):
            low = head * head_width // LANES
            high = ((head + 1) * head_width - 1) // LANES + 1
            window = slice(low * LANES, high * LANES)
            lane = lax.broadcasted_iota(jnp.int32, (rows, (high - low) * LANES), 1) + low * LANES
            mine = (lane >= head * head_width) & (lane < (head + 1) * head_width)
            zeros = jnp.zeros((rows, (high - low) * LANES), jnp.bfloat16)
            queries = jnp.where(mine, query[here, window], zeros)
            scores = lax.dot_general(
                queries, key[here, window], (((1,), (1,)), ((), ())), preferred_element_type=jnp.float32
            )
            scores = jnp.where(same, scores * scale, MASKED)
            powers = jnp.exp(scores - jnp.max(scores, axis=-1, keepdims=True))
            weights = powers * (1.0 / jnp.sum(powers, axis=-1, keepdims=True))
            values = jnp.where(mine, value[here, window], zeros)
            part = jnp.dot(weights.astype(jnp.bfloat16), values, preferred_element_type=jnp.float32)
            for block in range(low, high):
                piece = part[:, (block - low) * LANES : (block - low + 1) * LANES]
                sums[block] = piece if sums[block] is None else sums[block] + piece
        for block, total in enumerate(sums):
            normed[here, block * LANES : (block + 1) * LANES] = total.astype(jnp.bfloat16)

    copies[3].wait()

    @pl.loop(0, width // step)
    def _(n):
        part = pl.ds(pl.multiple_of(n * step, step), step)
        output = jnp.dot(normed[...], wo[:, part], preferred_element_type=jnp.float32)
        output = output + bias_ref[:, part]
        for group in range(groups):
            here = slice(group * rows, (group + 1) * rows)
            piece = (output[here] + held[here, part].astype(jnp.float32)).reshape(frames, 8, step)
            out_ref[:, group * 8 : group * 8 + 8, part] = piece.astype(jnp.bfloat16)


def attention(tokens, norm_gain, out_bias, w_query, w_key, w_value, w_out):
    sources, span, pixels, half_width = tokens.shape
    frames, width = sources * span // 2, 2 * half_width
    count = frames * pixels
    weight = pltpu.VMEM((width, width), jnp.bfloat16)
    rows = pltpu.VMEM((count, width), jnp.bfloat16)
    anywhere = pl.BlockSpec(memory_space=pl.ANY)
    inside = pl.BlockSpec(memory_space=pltpu.VMEM)
    return pl.pallas_call(
        attention_kernel,
        out_shape=jax.ShapeDtypeStruct((frames, pixels, width), jnp.bfloat16),
        in_specs=[inside, inside, inside, anywhere, anywhere, anywhere, anywhere],
        out_specs=inside,
        scratch_shapes=[weight] * 4 + [rows] * 5 + [pltpu.SemaphoreType.DMA((4,))],
        cost_estimate=pl.CostEstimate(
            flops=8 * count * width * width,
            bytes_accessed=8 * width * width + 4 * count * width,
            transcendentals=count * HEADS * frames * 8,
        ),
    )(
        tokens, norm_gain.reshape(1, width), out_bias.reshape(1, width), w_query, w_key, w_value, w_out
    )


def on_device(
    features,
    time_weight,
    time_bias,
    down_weight,
    down_bias,
    norm_gain,
    w_query,
    w_key,
    w_value,
    w_out,
    out_bias,
):
    frames_here, rows_here, columns, channels = features.shape
    groups = lax.axis_size("frame")
    lines = groups // 2
    frame, row = lax.axis_index("frame"), lax.axis_index("row")
    side = frame % 2

    everyone = range(groups)
    swapped = [(at, at ^ 1) for at in everyone]
    own = [
        lax.dynamic_slice_in_dim(features, jnp.where(side == 0, at, frames_here - 1 - at), 1, axis=0)
        for at in range(frames_here)
    ]
    other = [lax.ppermute(own[0], "frame", swapped)]
    later = list(own[1:])
    other[0], *later = lax.optimization_barrier([other[0]] + later)
    other += [lax.ppermute(value, "frame", swapped) for value in later]
    outward = [(at, at + (2 if at % 2 else -2)) for at in everyone]
    inward = [(at, at + (-2 if at % 2 else 2)) for at in everyone]
    inside = lambda pairs: [(source, target) for source, target in pairs if 0 <= target < groups]
    last = lax.ppermute(own[0], "frame", inside(outward))
    first = lax.ppermute(other[0], "frame", inside(inward))
    sequence = [first] + own + other[::-1] + [last]

    pieces, where, distant = strided_weights(down_weight, frame, row, channels)

    taps = jnp.where(side == 0, time_weight, time_weight[::-1])
    final = temporal(sequence, taps, time_bias, rows_here - 1, 1, 1)
    upper = passed_along(final, "row", 1)
    planes = temporal(sequence, taps, time_bias, 0, rows_here, 2)
    shares = down_bias.reshape(lines, 2, down_bias.shape[0] // groups)
    bias = lax.dynamic_index_in_dim(shares, side, axis=1, keepdims=False).reshape(-1)
    planes, *distant = lax.optimization_barrier([planes] + distant)
    pieces += [lax.ppermute(value, "row", [(at, at ^ 1) for at in range(lax.axis_size("row"))]) for value in distant]

    half_rows, half_cols = rows_here // 2, columns // 2
    pixels_here = half_rows * half_cols // groups
    chunks = 2 if groups == half_rows and pixels_here % 16 == 0 else 1
    results = []
    for coarse in strided(planes, upper, pieces, where, bias, chunks):
        half_width = coarse.shape[-1]
        part = pixels_here // chunks
        tokens = coarse
        if groups != half_rows:
            tokens = tokens.transpose(1, 0, 2, 3).reshape(2 * frames_here, groups, part, half_width)
            tokens = tokens.transpose(1, 0, 2, 3)
        moved = lax.all_to_all(tokens, "frame", split_axis=0, concat_axis=0, tiled=True)
        result = attention(moved, norm_gain, out_bias, w_query, w_key, w_value, w_out)
        result = result.reshape(groups, frames_here, part, 2 * half_width)
        results.append(lax.all_to_all(result, "frame", split_axis=0, concat_axis=0, tiled=True))
    returned = jnp.concatenate(results, axis=2).transpose(1, 0, 2, 3)
    return returned.reshape(frames_here, half_rows, half_cols, 2 * half_width)


def strided_weights(down_weight, frame, row, channels):
    groups, row_devices = lax.axis_size("frame"), lax.axis_size("row")
    lines = groups // 2
    share = down_weight.shape[3]
    line = frame // 2
    shard = down_weight.transpose(0, 1, 3, 2).reshape(9, share, channels)
    unit = share // 2
    if unit % 16 or lines & (lines - 1) or row_devices % 4:
        members = [[2 * at + side for at in range(lines)] for side in range(2)]
        gathered = lax.all_gather(shard, "frame", axis=1, tiled=True, axis_index_groups=members)
        return [gathered[:, None]], jnp.zeros((1, 2), jnp.int32), []
    core, plane = row % 2, row // 2 % 2
    shard = shard.reshape(9, 2, unit, channels)
    pieces, where, distant, beyond = [shard], [(0, 2 * line)], [], []
    mine = lax.dynamic_slice(shard, (4 * plane, core, 0, 0), (5, 1, unit, channels))
    rows = range(row_devices)
    for distance in range(1, lines):
        place = 2 * (line ^ distance)
        steps = [(at, (at // 2 ^ distance) * 2 + at % 2) for at in range(groups)]
        near = lax.ppermute(mine, "frame", steps)
        sent = lax.dynamic_slice_in_dim(near, plane, 4, axis=0)
        far = lax.ppermute(sent, "row", [(at, at ^ 2) for at in rows])
        pieces += [near, far, lax.ppermute(near, "row", [(at, at ^ 1) for at in rows])]
        where += [(4 * plane, place + core), (5 - 5 * plane, place + core), (4 * plane, place + 1 - core)]
        distant.append(far)
        beyond.append((5 - 5 * plane, place + 1 - core))
    where = jnp.stack([jnp.stack([jnp.int32(tap), jnp.int32(at)]) for tap, at in where + beyond])
    return pieces, where, distant


def solution(mesh):
    return jax.shard_map(
        on_device,
        mesh=mesh,
        in_specs=(
            P("frame", "row", None, None),
            P(),
            P(),
            P(None, None, None, "frame"),
            P(),
            P(),
            P(),
            P(),
            P(),
            P(),
            P(),
        ),
        out_specs=P("frame", "row", None, None),
        check_vma=False,
    )
```

```python
import functools

import jax
import jax.numpy as jnp
from jax import lax
from jax.experimental import pallas as pl
from jax.experimental.pallas import tpu as pltpu
from jax.sharding import PartitionSpec as P


HEADS = 16
LANES = 128
MASKED = -3.0e38


def passed_along(value, axis, steps):
    count = lax.axis_size(axis)
    leading, last = (max(0, -steps), min(count, count - steps))
    return lax.ppermute(value, axis, [(source, source + steps) for source in range(leading, last)])


def temporal_kernel(*refs):
    *frame_refs, weight_ref, bias_ref, out_ref, held = refs
    rows, columns, channels = frame_refs[0].shape[1:]
    frames = len(frame_refs) - 2
    count = rows * columns
    values = [ref[...].reshape(count, channels) for ref in frame_refs]
    stacked = [jnp.concatenate(values[tap : tap + frames], axis=0) for tap in range(3)]
    total = jnp.dot(jnp.concatenate(stacked, axis=1), weight_ref[...], preferred_element_type=jnp.float32)
    total = total + (stacked[1].astype(jnp.float32) + bias_ref[...])
    total = total.astype(jnp.bfloat16).astype(jnp.float32)
    lanes = channels // LANES
    for block in range(lanes):
        held[block, 8:, :] = total[:, block * LANES : (block + 1) * LANES]
    half = columns // 2
    first = lax.broadcasted_iota(jnp.int32, (rows * half, LANES), 0) % half == 0
    for place in range(frames):
        for block in range(lanes):
            begin = place * count
            moved = held[block, pl.ds(begin + 7, rows * half, stride=2), :]
            even = held[block, pl.ds(begin + 8, rows * half, stride=2), :]
            odd = held[block, pl.ds(begin + 9, rows * half, stride=2), :]
            moved = jnp.where(first, 0.0, moved)
            for tap, plane in enumerate((moved, even, odd)):
                start = tap * channels + block * LANES
                out_ref[:, place, :, start : start + LANES] = plane.astype(jnp.bfloat16).reshape(
                    rows, half, LANES
                )


def from_row(step, start, columns, channels):
    return pl.BlockSpec((1, step, columns, channels), lambda r: (0, r + start // step, 0, 0))


def temporal(sequence, time_weight, time_bias, start, rows, step):
    _, _, columns, channels = sequence[0].shape
    frames = len(sequence) - 2
    half = columns // 2
    return pl.pallas_call(
        temporal_kernel,
        out_shape=jax.ShapeDtypeStruct((rows, frames, half, 3 * channels), jnp.bfloat16),
        grid=(rows // step,),
        in_specs=[from_row(step, start, columns, channels)] * len(sequence)
        + [
            pl.BlockSpec((3 * channels, channels), lambda r: (0, 0)),
            pl.BlockSpec((1, channels), lambda r: (0, 0)),
        ],
        out_specs=pl.BlockSpec((step, frames, half, 3 * channels), lambda r: (r, 0, 0, 0)),
        scratch_shapes=[pltpu.VMEM((channels // LANES, 8 + frames * step * columns, LANES), jnp.float32)],
        cost_estimate=pl.CostEstimate(
            flops=6 * frames * rows * columns * channels * channels,
            bytes_accessed=2 * (5 * frames + 2) * rows * columns * channels,
            transcendentals=0,
        ),
    )(*sequence, time_weight.reshape(3 * channels, channels), time_bias.reshape(1, channels))


def strided_kernel(spans, parts, where_ref, upper_ref, bias_ref, *refs):
    planes_refs, refs = refs[:parts], refs[parts:]
    pieces, (*out_refs, weight, total, sems) = refs[: len(spans)], refs[len(spans) :]
    step = pl.program_id(0)
    _, _, frames, half_cols, width = planes_refs[0].shape
    half_rows = sum(ref.shape[0] for ref in planes_refs)
    count = half_rows * frames * half_cols
    channels = width // 3
    _, units, unit, _ = weight.shape

    def load(place, piece, run, at):
        tap = where_ref[place, 0] + at
        lanes = pl.ds(pl.multiple_of(tap % 3 * channels, LANES), channels)
        target = weight.at[tap // 3, pl.ds(where_ref[place, 1], run), :, lanes]
        pltpu.make_async_copy(piece.at[at], target, sems.at[tap // 3]).start()

    def product(values, tap):
        pltpu.make_async_copy(weight.at[tap], weight.at[tap], sems.at[tap]).wait()
        return lax.dot_general(
            values.reshape(count, width),
            weight[tap].reshape(units * unit, width),
            (((1,), (1,)), ((), ())),
            preferred_element_type=jnp.float32,
        )

    @pl.when(step == 0)
    def _():
        for place, (piece, (taps, run)) in enumerate(zip(pieces, spans)):
            for at in range(taps):
                load(place, piece, run, at)
        values = jnp.concatenate([upper_ref[...]] + [ref[:, 0] for ref in planes_refs], axis=0)[:half_rows]
        total[...] = product(values, 0) + bias_ref[...]

    @pl.when(step == 1)
    def _():
        total[...] += product(jnp.concatenate([ref[:, 0] for ref in planes_refs], axis=0), 2)

    @pl.when(step == 2)
    def _():
        done = total[...] + product(jnp.concatenate([ref[:, 0] for ref in planes_refs], axis=0), 1)
        done = done.reshape(half_rows, frames, half_cols, done.shape[1])
        part = half_cols // len(out_refs)
        for chunk, out_ref in enumerate(out_refs):
            out_ref[...] = done[:, :, chunk * part : (chunk + 1) * part].astype(jnp.bfloat16)


def strided(planes, upper, pieces, where, bias, chunks):
    _, frames, half_cols, width = planes[0].shape
    outputs = bias.shape[0]
    half_rows = sum(part.shape[0] for part in planes) // 2
    count = half_rows * frames * half_cols
    unit = pieces[0].shape[2]
    block = (half_rows, frames, half_cols // chunks, outputs)
    anywhere = pl.BlockSpec(memory_space=pl.ANY)
    return pl.pallas_call(
        functools.partial(strided_kernel, tuple(piece.shape[:2] for piece in pieces), len(planes)),
        out_shape=[jax.ShapeDtypeStruct(block, jnp.bfloat16)] * chunks,
        grid=(3,),
        in_specs=[
            pl.BlockSpec(memory_space=pltpu.SMEM),
            pl.BlockSpec((1, frames, half_cols, width), lambda a: (0, 0, 0, 0)),
            pl.BlockSpec((1, outputs), lambda a: (0, 0)),
        ]
        + [
            pl.BlockSpec(
                (part.shape[0] // 2, 1, frames, half_cols, width), lambda a: (0, 1 - a // 2, 0, 0, 0)
            )
            for part in planes
        ]
        + [anywhere] * len(pieces),
        out_specs=[pl.BlockSpec(block, lambda a: (0, 0, 0, 0))] * chunks,
        scratch_shapes=[
            pltpu.VMEM((3, outputs // unit, unit, width), jnp.bfloat16),
            pltpu.VMEM((count, outputs), jnp.float32),
            pltpu.SemaphoreType.DMA((3,)),
        ],
        cost_estimate=pl.CostEstimate(
            flops=6 * count * width * outputs,
            bytes_accessed=2 * (2 * count * width + 3 * width * outputs + count * outputs),
            transcendentals=0,
        ),
    )(
        where,
        upper,
        bias.reshape(1, outputs),
        *(part.reshape(-1, 2, frames, half_cols, width) for part in planes),
        *pieces,
    )


def attention_kernel(
    tokens_ref, gain_ref, bias_ref, wq_hbm, wk_hbm, wv_hbm, wo_hbm, out_ref,
    wq, wk, wv, wo, held, normed, query, key, value, scores, weights, sems,
):
    copies = []
    for place, (source, target) in enumerate(((wq_hbm, wq), (wk_hbm, wk), (wv_hbm, wv), (wo_hbm, wo))):
        copies.append(pltpu.make_async_copy(source, target, sems.at[place]))
        copies[-1].start()
    frames, pixels, width = out_ref.shape
    groups = pixels // 8
    rows = frames * 8
    sources, span, _, half_width = tokens_ref.shape
    share = half_width // (sources // 2)
    head_width = width // HEADS
    scale = head_width ** (-0.5)
    for group in range(groups):
        here = slice(group * 8, group * 8 + 8)
        low = [tokens_ref[2 * line, :, here, :] for line in range(sources // 2)]
        high = [tokens_ref[2 * line + 1, span - 1 - at, here, :] for line in range(sources // 2) for at in range(span)]
        low = jnp.concatenate([value.astype(jnp.float32).reshape(span * 8, half_width) for value in low], axis=0)
        high = jnp.concatenate([value.astype(jnp.float32) for value in high], axis=0)
        parts = []
        for line in range(sources // 2):
            parts += [low[:, line * share : (line + 1) * share], high[:, line * share : (line + 1) * share]]
        tokens = jnp.concatenate(parts, axis=1)
        held[group * rows : (group + 1) * rows, :] = tokens.astype(jnp.bfloat16)
        centred = tokens - jnp.mean(tokens, axis=-1, keepdims=True)
        spread = jnp.mean(centred * centred, axis=-1, keepdims=True)
        result = centred * lax.rsqrt(spread + 1e-05) * gain_ref[...]
        normed[group * rows : (group + 1) * rows, :] = result.astype(jnp.bfloat16)
    for place, (weight, target) in enumerate(((wq, query), (wk, key), (wv, value))):
        copies[place].wait()
        target[...] = jnp.dot(normed[...], weight[...], preferred_element_type=jnp.float32).astype(jnp.bfloat16)

    same = (
        lax.broadcasted_iota(jnp.int32, (rows, rows), 0) % 8
        == lax.broadcasted_iota(jnp.int32, (rows, rows), 1) % 8
    )
    windows = []
    for head in range(HEADS):
        low = head * head_width // LANES
        high = ((head + 1) * head_width - 1) // LANES + 1
        lane = lax.broadcasted_iota(jnp.int32, (rows, (high - low) * LANES), 1) + low * LANES
        mine = (lane >= head * head_width) & (lane < (head + 1) * head_width)
        windows.append((low, high, mine))

    for group in range(groups):
        here = slice(group * rows, (group + 1) * rows)
        for head, (low, high, mine) in enumerate(windows):
            window = slice(low * LANES, high * LANES)
            queries = jnp.where(mine, query[here, window], jnp.zeros(mine.shape, jnp.bfloat16))
            scores[head] = lax.dot_general(
                queries, key[here, window], (((1,), (1,)), ((), ())), preferred_element_type=jnp.float32
            )

        @pl.loop(0, HEADS // 4)
        def _(quarter):
            part = pl.ds(quarter * 4, 4)
            some = jnp.where(same[None], scores[part] * scale, MASKED)
            powers = jnp.exp(some - jnp.max(some, axis=-1, keepdims=True))
            share_of = 1.0 / jnp.sum(powers, axis=-1, keepdims=True)
            weights[part] = (powers * share_of).astype(jnp.bfloat16)

        sums = [None] * (width // LANES)
        for head, (low, high, mine) in enumerate(windows):
            window = slice(low * LANES, high * LANES)
            values = jnp.where(mine, value[here, window], jnp.zeros(mine.shape, jnp.bfloat16))
            part = jnp.dot(weights[head], values, preferred_element_type=jnp.float32)
            for block in range(low, high):
                piece = part[:, (block - low) * LANES : (block - low + 1) * LANES]
                sums[block] = piece if sums[block] is None else sums[block] + piece
        for block, total in enumerate(sums):
            normed[here, block * LANES : (block + 1) * LANES] = total.astype(jnp.bfloat16)

    copies[3].wait()
    output = jnp.dot(normed[...], wo[...], preferred_element_type=jnp.float32)
    output = output + bias_ref[...] + held[...].astype(jnp.float32)
    for group in range(groups):
        piece = output[group * rows : (group + 1) * rows].reshape(frames, 8, width)
        out_ref[:, group * 8 : group * 8 + 8, :] = piece.astype(jnp.bfloat16)


def attention(tokens, norm_gain, out_bias, w_query, w_key, w_value, w_out):
    sources, span, pixels, half_width = tokens.shape
    frames, width = sources * span // 2, 2 * half_width
    count = frames * pixels
    weight = pltpu.VMEM((width, width), jnp.bfloat16)
    rows = pltpu.VMEM((count, width), jnp.bfloat16)
    anywhere = pl.BlockSpec(memory_space=pl.ANY)
    inside = pl.BlockSpec(memory_space=pltpu.VMEM)
    return pl.pallas_call(
        attention_kernel,
        out_shape=jax.ShapeDtypeStruct((frames, pixels, width), jnp.bfloat16),
        in_specs=[inside, inside, inside, anywhere, anywhere, anywhere, anywhere],
        out_specs=inside,
        scratch_shapes=[weight] * 4
        + [rows] * 5
        + [
            pltpu.VMEM((HEADS, frames * 8, frames * 8), jnp.float32),
            pltpu.VMEM((HEADS, frames * 8, frames * 8), jnp.bfloat16),
            pltpu.SemaphoreType.DMA((4,)),
        ],
        cost_estimate=pl.CostEstimate(
            flops=8 * count * width * width,
            bytes_accessed=8 * width * width + 4 * count * width,
            transcendentals=count * HEADS * frames * 8,
        ),
    )(
        tokens, norm_gain.reshape(1, width), out_bias.reshape(1, width), w_query, w_key, w_value, w_out
    )


def on_device(
    features,
    time_weight,
    time_bias,
    down_weight,
    down_bias,
    norm_gain,
    w_query,
    w_key,
    w_value,
    w_out,
    out_bias,
):
    frames_here, rows_here, columns, channels = features.shape
    groups = lax.axis_size("frame")
    lines = groups // 2
    frame, row = lax.axis_index("frame"), lax.axis_index("row")
    side = frame % 2

    everyone = range(groups)
    swapped = [(at, at ^ 1) for at in everyone]
    outward = [(at, at + (2 if at % 2 else -2)) for at in everyone]
    inward = [(at, at + (-2 if at % 2 else 2)) for at in everyone]
    inside = lambda pairs: [(source, target) for source, target in pairs if 0 <= target < groups]
    half = rows_here // 2
    starts = (half, 0)

    def own_frame(at, start):
        place = jnp.where(side == 0, at, frames_here - 1 - at)
        return lax.dynamic_slice(features, (place, start, 0, 0), (1, half, columns, channels))

    def moved_along(value, pairs):
        return lax.ppermute(value, "frame", pairs)

    own = [[own_frame(at, start) for at in range(frames_here)] for start in starts]
    outer = [moved_along(value[0], swapped) for value in own]
    last = [moved_along(value[0], inside(outward)) for value in own]
    first = [moved_along(value, inside(inward)) for value in outer]
    inner = [[moved_along(each, swapped) for each in value[1:]] for value in own]
    sequences = [
        [first[part]] + own[part] + inner[part][::-1] + [outer[part], last[part]] for part in range(len(starts))
    ]

    pieces, where, distant = strided_weights(down_weight, frame, row, channels)

    taps = jnp.where(side == 0, time_weight, time_weight[::-1])
    final = temporal(sequences[0], taps, time_bias, half - 1, 1, 1)
    upper = passed_along(final, "row", 1)
    lower_planes = temporal(sequences[0], taps, time_bias, 0, half, 2)
    upper_planes = temporal(sequences[1], taps, time_bias, 0, half, 2)
    lower_planes, *distant = lax.optimization_barrier([lower_planes] + distant)
    planes = [upper_planes, lower_planes]
    shares = down_bias.reshape(lines, 2, down_bias.shape[0] // groups)
    bias = lax.dynamic_index_in_dim(shares, side, axis=1, keepdims=False).reshape(-1)
    pieces += [lax.ppermute(value, "row", [(at, at ^ 1) for at in range(lax.axis_size("row"))]) for value in distant]

    half_rows, half_cols = rows_here // 2, columns // 2
    pixels_here = half_rows * half_cols // groups
    chunks = 2 if groups == half_rows and pixels_here % 16 == 0 else 1
    moved, results = [], []
    part = pixels_here // chunks
    for coarse in strided(planes, upper, pieces, where, bias, chunks):
        half_width = coarse.shape[-1]
        tokens = coarse
        if groups != half_rows:
            tokens = tokens.transpose(1, 0, 2, 3).reshape(2 * frames_here, groups, part, half_width)
            tokens = tokens.transpose(1, 0, 2, 3)
        moved.append(lax.all_to_all(tokens, "frame", split_axis=0, concat_axis=0, tiled=True))
    for tokens in moved:
        result = attention(tokens, norm_gain, out_bias, w_query, w_key, w_value, w_out)
        result = result.reshape(groups, frames_here, part, 2 * half_width)
        results.append(lax.all_to_all(result, "frame", split_axis=0, concat_axis=0, tiled=True))
    returned = jnp.concatenate(results, axis=2).transpose(1, 0, 2, 3)
    return returned.reshape(frames_here, half_rows, half_cols, 2 * half_width)


def strided_weights(down_weight, frame, row, channels):
    groups, row_devices = lax.axis_size("frame"), lax.axis_size("row")
    lines = groups // 2
    share = down_weight.shape[3]
    line = frame // 2
    shard = down_weight.transpose(0, 1, 3, 2).reshape(9, share, channels)
    unit = share // 2
    if unit % 16 or lines & (lines - 1) or row_devices % 4:
        members = [[2 * at + side for at in range(lines)] for side in range(2)]
        gathered = lax.all_gather(shard, "frame", axis=1, tiled=True, axis_index_groups=members)
        return [gathered[:, None]], jnp.zeros((1, 2), jnp.int32), []
    core, plane = row % 2, row // 2 % 2
    shard = shard.reshape(9, 2, unit, channels)
    pieces, where, distant, beyond = [shard], [(0, 2 * line)], [], []
    mine = lax.dynamic_slice(shard, (4 * plane, core, 0, 0), (5, 1, unit, channels))
    rows = range(row_devices)
    for distance in range(1, lines):
        place = 2 * (line ^ distance)
        steps = [(at, (at // 2 ^ distance) * 2 + at % 2) for at in range(groups)]
        near = lax.ppermute(mine, "frame", steps)
        sent = lax.dynamic_slice_in_dim(near, plane, 4, axis=0)
        far = lax.ppermute(sent, "row", [(at, at ^ 2) for at in rows])
        pieces += [near, far, lax.ppermute(near, "row", [(at, at ^ 1) for at in rows])]
        where += [(4 * plane, place + core), (5 - 5 * plane, place + core), (4 * plane, place + 1 - core)]
        distant.append(far)
        beyond.append((5 - 5 * plane, place + 1 - core))
    where = jnp.stack([jnp.stack([jnp.int32(tap), jnp.int32(at)]) for tap, at in where + beyond])
    return pieces, where, distant


def solution(mesh):
    return jax.shard_map(
        on_device,
        mesh=mesh,
        in_specs=(
            P("frame", "row", None, None),
            P(),
            P(),
            P(None, None, None, "frame"),
            P(),
            P(),
            P(),
            P(),
            P(),
            P(),
            P(),
        ),
        out_specs=P("frame", "row", None, None),
        check_vma=False,
    )
```

```python
import functools

import jax
import jax.numpy as jnp
from jax import lax
from jax.experimental import pallas as pl
from jax.experimental.pallas import tpu as pltpu
from jax.sharding import PartitionSpec as P


HEADS = 16
LANES = 128
MASKED = -3.0e38


def passed_along(value, axis, steps):
    count = lax.axis_size(axis)
    leading, last = (max(0, -steps), min(count, count - steps))
    return lax.ppermute(value, axis, [(source, source + steps) for source in range(leading, last)])


def temporal_kernel(*refs):
    *frame_refs, weight_ref, bias_ref, out_ref, held = refs
    rows, columns, channels = frame_refs[0].shape[1:]
    frames = len(frame_refs) - 2
    count = rows * columns
    values = [ref[...].reshape(count, channels) for ref in frame_refs]
    stacked = [jnp.concatenate(values[tap : tap + frames], axis=0) for tap in range(3)]
    total = jnp.dot(jnp.concatenate(stacked, axis=1), weight_ref[...], preferred_element_type=jnp.float32)
    total = total + (stacked[1].astype(jnp.float32) + bias_ref[...])
    total = total.astype(jnp.bfloat16).astype(jnp.float32)
    lanes = channels // LANES
    for block in range(lanes):
        held[block, 8:, :] = total[:, block * LANES : (block + 1) * LANES]
    half = columns // 2
    first = lax.broadcasted_iota(jnp.int32, (rows * half, LANES), 0) % half == 0
    for place in range(frames):
        for block in range(lanes):
            begin = place * count
            moved = held[block, pl.ds(begin + 7, rows * half, stride=2), :]
            even = held[block, pl.ds(begin + 8, rows * half, stride=2), :]
            odd = held[block, pl.ds(begin + 9, rows * half, stride=2), :]
            moved = jnp.where(first, 0.0, moved)
            for tap, plane in enumerate((moved, even, odd)):
                start = tap * channels + block * LANES
                out_ref[:, place, :, start : start + LANES] = plane.astype(jnp.bfloat16).reshape(
                    rows, half, LANES
                )


def from_row(step, start, columns, channels):
    return pl.BlockSpec((1, step, columns, channels), lambda r: (0, r + start // step, 0, 0))


def temporal(sequence, time_weight, time_bias, start, rows, step):
    _, _, columns, channels = sequence[0].shape
    frames = len(sequence) - 2
    half = columns // 2
    return pl.pallas_call(
        temporal_kernel,
        out_shape=jax.ShapeDtypeStruct((rows, frames, half, 3 * channels), jnp.bfloat16),
        grid=(rows // step,),
        in_specs=[from_row(step, start, columns, channels)] * len(sequence)
        + [
            pl.BlockSpec((3 * channels, channels), lambda r: (0, 0)),
            pl.BlockSpec((1, channels), lambda r: (0, 0)),
        ],
        out_specs=pl.BlockSpec((step, frames, half, 3 * channels), lambda r: (r, 0, 0, 0)),
        scratch_shapes=[pltpu.VMEM((channels // LANES, 8 + frames * step * columns, LANES), jnp.float32)],
        cost_estimate=pl.CostEstimate(
            flops=6 * frames * rows * columns * channels * channels,
            bytes_accessed=2 * (5 * frames + 2) * rows * columns * channels,
            transcendentals=0,
        ),
    )(*sequence, time_weight.reshape(3 * channels, channels), time_bias)


def strided_kernel(spans, parts, where_ref, upper_ref, bias_ref, *refs):
    planes_refs, refs = refs[:parts], refs[parts:]
    pieces, (out_ref, weight, total, sems) = refs[: len(spans)], refs[len(spans) :]
    step = pl.program_id(0)
    _, _, frames, half_cols, width = planes_refs[0].shape
    half_rows = sum(ref.shape[0] for ref in planes_refs)
    count = half_rows * frames * half_cols
    channels = width // 3
    _, units, unit, _ = weight.shape

    def load(place, piece, run, at):
        tap = where_ref[place, 0] + at
        lanes = pl.ds(pl.multiple_of(tap % 3 * channels, LANES), channels)
        target = weight.at[tap // 3, pl.ds(where_ref[place, 1], run), :, lanes]
        pltpu.make_async_copy(piece.at[at], target, sems.at[tap // 3]).start()

    def product(values, tap):
        pltpu.make_async_copy(weight.at[tap], weight.at[tap], sems.at[tap]).wait()
        return lax.dot_general(
            values.reshape(count, width),
            weight[tap].reshape(units * unit, width),
            (((1,), (1,)), ((), ())),
            preferred_element_type=jnp.float32,
        )

    @pl.when(step == 0)
    def _():
        for place, (piece, (taps, run)) in enumerate(zip(pieces, spans)):
            for at in range(taps):
                load(place, piece, run, at)
        values = jnp.concatenate([upper_ref[...]] + [ref[:, 0] for ref in planes_refs], axis=0)[:half_rows]
        total[...] = product(values, 0) + bias_ref[...]

    @pl.when(step == 1)
    def _():
        total[...] += product(jnp.concatenate([ref[:, 0] for ref in planes_refs], axis=0), 2)

    @pl.when(step == 2)
    def _():
        done = total[...] + product(jnp.concatenate([ref[:, 0] for ref in planes_refs], axis=0), 1)
        out_ref[...] = done.astype(jnp.bfloat16).reshape(out_ref.shape)


def strided(planes, upper, pieces, where, bias, chunk, chunks):
    _, frames, all_cols, width = planes[0].shape
    half_cols = all_cols // chunks
    outputs = bias.shape[0]
    half_rows = sum(part.shape[0] for part in planes) // 2
    count = half_rows * frames * half_cols
    unit = pieces[0].shape[2]
    block = (half_rows, frames, half_cols, outputs)
    anywhere = pl.BlockSpec(memory_space=pl.ANY)
    return pl.pallas_call(
        functools.partial(strided_kernel, tuple(piece.shape[:2] for piece in pieces), len(planes)),
        out_shape=jax.ShapeDtypeStruct(block, jnp.bfloat16),
        grid=(3,),
        in_specs=[
            pl.BlockSpec(memory_space=pltpu.SMEM),
            pl.BlockSpec((1, frames, half_cols, width), lambda a: (0, 0, chunk, 0)),
            pl.BlockSpec((1, outputs), lambda a: (0, 0)),
        ]
        + [
            pl.BlockSpec(
                (part.shape[0] // 2, 1, frames, half_cols, width), lambda a: (0, 1 - a // 2, 0, chunk, 0)
            )
            for part in planes
        ]
        + [anywhere] * len(pieces),
        out_specs=pl.BlockSpec(block, lambda a: (0, 0, 0, 0)),
        scratch_shapes=[
            pltpu.VMEM((3, outputs // unit, unit, width), jnp.bfloat16),
            pltpu.VMEM((count, outputs), jnp.float32),
            pltpu.SemaphoreType.DMA((3,)),
        ],
        cost_estimate=pl.CostEstimate(
            flops=6 * count * width * outputs,
            bytes_accessed=2 * (2 * count * width + 3 * width * outputs + count * outputs),
            transcendentals=0,
        ),
    )(
        where,
        upper,
        bias.reshape(1, outputs),
        *(part.reshape(-1, 2, frames, all_cols, width) for part in planes),
        *pieces,
    )


def attention_kernel(
    tokens_ref, gain_ref, bias_ref, wq_hbm, wk_hbm, wv_hbm, wo_hbm, out_ref,
    wq, wk, wv, wo, held, normed, query, key, value, scores, weights, sems,
):
    copies = []
    for place, (source, target) in enumerate(((wq_hbm, wq), (wk_hbm, wk), (wv_hbm, wv), (wo_hbm, wo))):
        copies.append(pltpu.make_async_copy(source, target, sems.at[place]))
        copies[-1].start()
    frames, pixels, width = out_ref.shape
    groups = pixels // 8
    rows = frames * 8
    sources, span, _, half_width = tokens_ref.shape
    share = half_width // (sources // 2)
    head_width = width // HEADS
    scale = head_width ** (-0.5)
    for group in range(groups):
        here = slice(group * 8, group * 8 + 8)
        low = [tokens_ref[2 * line, :, here, :] for line in range(sources // 2)]
        high = [tokens_ref[2 * line + 1, span - 1 - at, here, :] for line in range(sources // 2) for at in range(span)]
        low = jnp.concatenate([value.astype(jnp.float32).reshape(span * 8, half_width) for value in low], axis=0)
        high = jnp.concatenate([value.astype(jnp.float32) for value in high], axis=0)
        parts = []
        for line in range(sources // 2):
            parts += [low[:, line * share : (line + 1) * share], high[:, line * share : (line + 1) * share]]
        tokens = jnp.concatenate(parts, axis=1)
        held[group * rows : (group + 1) * rows, :] = tokens.astype(jnp.bfloat16)
        centred = tokens - jnp.mean(tokens, axis=-1, keepdims=True)
        spread = jnp.mean(centred * centred, axis=-1, keepdims=True)
        result = centred * lax.rsqrt(spread + 1e-05) * gain_ref[...]
        normed[group * rows : (group + 1) * rows, :] = result.astype(jnp.bfloat16)
    for place, (weight, target) in enumerate(((wq, query), (wk, key), (wv, value))):
        copies[place].wait()
        target[...] = jnp.dot(normed[...], weight[...], preferred_element_type=jnp.float32).astype(jnp.bfloat16)

    same = (
        lax.broadcasted_iota(jnp.int32, (rows, rows), 0) % 8
        == lax.broadcasted_iota(jnp.int32, (rows, rows), 1) % 8
    )
    windows = []
    for head in range(HEADS):
        low = head * head_width // LANES
        high = ((head + 1) * head_width - 1) // LANES + 1
        lane = lax.broadcasted_iota(jnp.int32, (rows, (high - low) * LANES), 1) + low * LANES
        mine = (lane >= head * head_width) & (lane < (head + 1) * head_width)
        windows.append((low, high, mine))

    for group in range(groups):
        here = slice(group * rows, (group + 1) * rows)
        for head, (low, high, mine) in enumerate(windows):
            window = slice(low * LANES, high * LANES)
            queries = jnp.where(mine, query[here, window], jnp.zeros(mine.shape, jnp.bfloat16))
            scores[head] = lax.dot_general(
                queries, key[here, window], (((1,), (1,)), ((), ())), preferred_element_type=jnp.float32
            )

        @pl.loop(0, HEADS // 4)
        def _(quarter):
            part = pl.ds(quarter * 4, 4)
            some = jnp.where(same[None], scores[part] * scale, MASKED)
            powers = jnp.exp(some - jnp.max(some, axis=-1, keepdims=True))
            share_of = 1.0 / jnp.sum(powers, axis=-1, keepdims=True)
            weights[part] = (powers * share_of).astype(jnp.bfloat16)

        sums = [None] * (width // LANES)
        for head, (low, high, mine) in enumerate(windows):
            window = slice(low * LANES, high * LANES)
            values = jnp.where(mine, value[here, window], jnp.zeros(mine.shape, jnp.bfloat16))
            part = jnp.dot(weights[head], values, preferred_element_type=jnp.float32)
            for block in range(low, high):
                piece = part[:, (block - low) * LANES : (block - low + 1) * LANES]
                sums[block] = piece if sums[block] is None else sums[block] + piece
        for block, total in enumerate(sums):
            normed[here, block * LANES : (block + 1) * LANES] = total.astype(jnp.bfloat16)

    copies[3].wait()
    output = jnp.dot(normed[...], wo[...], preferred_element_type=jnp.float32)
    output = output + bias_ref[...] + held[...].astype(jnp.float32)
    for group in range(groups):
        piece = output[group * rows : (group + 1) * rows].reshape(frames, 8, width)
        out_ref[:, group * 8 : group * 8 + 8, :] = piece.astype(jnp.bfloat16)


def attention(tokens, norm_gain, out_bias, w_query, w_key, w_value, w_out):
    sources, span, pixels, half_width = tokens.shape
    frames, width = sources * span // 2, 2 * half_width
    count = frames * pixels
    weight = pltpu.VMEM((width, width), jnp.bfloat16)
    rows = pltpu.VMEM((count, width), jnp.bfloat16)
    anywhere = pl.BlockSpec(memory_space=pl.ANY)
    inside = pl.BlockSpec(memory_space=pltpu.VMEM)
    return pl.pallas_call(
        attention_kernel,
        out_shape=jax.ShapeDtypeStruct((frames, pixels, width), jnp.bfloat16),
        in_specs=[inside, inside, inside, anywhere, anywhere, anywhere, anywhere],
        out_specs=inside,
        scratch_shapes=[weight] * 4
        + [rows] * 5
        + [
            pltpu.VMEM((HEADS, frames * 8, frames * 8), jnp.float32),
            pltpu.VMEM((HEADS, frames * 8, frames * 8), jnp.bfloat16),
            pltpu.SemaphoreType.DMA((4,)),
        ],
        cost_estimate=pl.CostEstimate(
            flops=8 * count * width * width,
            bytes_accessed=8 * width * width + 4 * count * width,
            transcendentals=count * HEADS * frames * 8,
        ),
    )(
        tokens, norm_gain.reshape(1, width), out_bias.reshape(1, width), w_query, w_key, w_value, w_out
    )


def on_device(
    features,
    time_weight,
    time_bias,
    down_weight,
    down_bias,
    norm_gain,
    w_query,
    w_key,
    w_value,
    w_out,
    out_bias,
):
    frames_here, rows_here, columns, channels = features.shape
    groups = lax.axis_size("frame")
    lines = groups // 2
    frame, row = lax.axis_index("frame"), lax.axis_index("row")
    side = frame % 2

    everyone = range(groups)
    swapped = [(at, at ^ 1) for at in everyone]
    outward = [(at, at + (2 if at % 2 else -2)) for at in everyone]
    inward = [(at, at + (-2 if at % 2 else 2)) for at in everyone]
    inside = lambda pairs: [(source, target) for source, target in pairs if 0 <= target < groups]
    half = rows_here // 2
    starts = (half, 0)

    def own_frame(at, start):
        place = jnp.where(side == 0, at, frames_here - 1 - at)
        return lax.dynamic_slice(features, (place, start, 0, 0), (1, half, columns, channels))

    def moved_along(value, pairs):
        return lax.ppermute(value, "frame", pairs)

    own = [[own_frame(at, start) for at in range(frames_here)] for start in starts]
    outer = [moved_along(value[0], swapped) for value in own]
    last = [moved_along(value[0], inside(outward)) for value in own]
    first = [moved_along(value, inside(inward)) for value in outer]
    inner = [[moved_along(each, swapped) for each in value[1:]] for value in own]
    sequences = [
        [first[part]] + own[part] + inner[part][::-1] + [outer[part], last[part]] for part in range(len(starts))
    ]

    pieces, where = strided_weights(down_weight, frame, row, channels)

    taps = jnp.where(side == 0, time_weight, time_weight[::-1])
    bias_row = time_bias.reshape(1, channels)
    lower_planes = temporal(sequences[0], taps, bias_row, 0, half, 2)
    upper = passed_along(lower_planes[-1:], "row", 1)
    upper_planes = temporal(sequences[1], taps, bias_row, 0, half, 2)
    planes = [upper_planes, lower_planes]
    shares = down_bias.reshape(lines, 2, down_bias.shape[0] // groups)
    bias = lax.dynamic_index_in_dim(shares, side, axis=1, keepdims=False).reshape(-1)

    half_rows, half_cols = rows_here // 2, columns // 2
    pixels_here = half_rows * half_cols // groups
    chunks = 2 if groups == half_rows and pixels_here % 16 == 0 else 1
    moved, results = [], []
    part = pixels_here // chunks
    for at in range(chunks):
        coarse = strided(planes, upper, pieces, where, bias, at, chunks)
        half_width = coarse.shape[-1]
        tokens = coarse
        if groups != half_rows:
            tokens = tokens.transpose(1, 0, 2, 3).reshape(2 * frames_here, groups, part, half_width)
            tokens = tokens.transpose(1, 0, 2, 3)
        moved.append(lax.all_to_all(tokens, "frame", split_axis=0, concat_axis=0, tiled=True))
    for tokens in moved:
        result = attention(tokens, norm_gain, out_bias, w_query, w_key, w_value, w_out)
        result = result.reshape(groups, frames_here, part, 2 * half_width)
        results.append(lax.all_to_all(result, "frame", split_axis=0, concat_axis=0, tiled=True))
    returned = jnp.concatenate(results, axis=2).transpose(1, 0, 2, 3)
    return returned.reshape(frames_here, half_rows, half_cols, 2 * half_width)


def strided_weights(down_weight, frame, row, channels):
    groups, row_devices = lax.axis_size("frame"), lax.axis_size("row")
    lines = groups // 2
    share = down_weight.shape[3]
    line = frame // 2
    shard = down_weight.transpose(0, 1, 3, 2).reshape(9, share, channels)
    unit = share // 2
    if unit % 16 or lines & (lines - 1) or row_devices % 4:
        members = [[2 * at + side for at in range(lines)] for side in range(2)]
        gathered = lax.all_gather(shard, "frame", axis=1, tiled=True, axis_index_groups=members)
        return [gathered[:, None]], jnp.zeros((1, 2), jnp.int32)
    core, plane = row % 2, row // 2 % 2
    shard = shard.reshape(9, 2, unit, channels)
    pieces, where = [shard], [(0, 2 * line)]
    mine = lax.dynamic_slice(shard, (4 * plane, core, 0, 0), (5, 1, unit, channels))
    rows = range(row_devices)

    def along(value, pairs):
        steps = [(2 * source + at, 2 * target + at) for source, target in pairs for at in range(2)]
        return lax.ppermute(value, "frame", steps)

    nears = {}
    for distance in range(1, lines):
        place = 2 * (line ^ distance)
        if lines == 4 and distance == 3:
            middle = along(mine, [(1, 2), (2, 1)])
            near = middle + along(nears[2], [(1, 0), (2, 3)])
        else:
            near = along(mine, [(at, at ^ distance) for at in range(lines)])
        nears[distance] = near
        sent = lax.dynamic_slice_in_dim(near, plane, 4, axis=0)
        far = lax.ppermute(sent, "row", [(at, at ^ 2) for at in rows])
        pieces += [near, far]
        where += [(4 * plane, place + core), (5 - 5 * plane, place + core)]
        for value, tap in ((near, 4 * plane), (far, 5 - 5 * plane)):
            pieces.append(lax.ppermute(value, "row", [(at, at ^ 1) for at in rows]))
            where.append((tap, place + 1 - core))
    return pieces, jnp.stack([jnp.stack([jnp.int32(tap), jnp.int32(at)]) for tap, at in where])


def solution(mesh):
    return jax.shard_map(
        on_device,
        mesh=mesh,
        in_specs=(
            P("frame", "row", None, None),
            P(),
            P(),
            P(None, None, None, "frame"),
            P(),
            P(),
            P(),
            P(),
            P(),
            P(),
            P(),
        ),
        out_specs=P("frame", "row", None, None),
        check_vma=False,
    )
```

```python
import functools

import jax
import jax.numpy as jnp
import numpy as np
from jax import lax
from jax.experimental import pallas as pl
from jax.experimental.pallas import tpu as pltpu
from jax.sharding import PartitionSpec as P


HEADS = 16
LANES = 128
MASKED = -3.0e38


def passed_along(value, axis, steps):
    count = lax.axis_size(axis)
    leading, last = (max(0, -steps), min(count, count - steps))
    return lax.ppermute(value, axis, [(source, source + steps) for source in range(leading, last)])


def temporal_kernel(*refs):
    *frame_refs, weight_ref, bias_ref, out_ref, held = refs
    rows, columns, channels = frame_refs[0].shape[1:]
    frames = len(frame_refs) - 2
    count = rows * columns
    values = [ref[...].reshape(count, channels) for ref in frame_refs]
    stacked = [jnp.concatenate(values[tap : tap + frames], axis=0) for tap in range(3)]
    total = jnp.dot(jnp.concatenate(stacked, axis=1), weight_ref[...], preferred_element_type=jnp.float32)
    total = total + (stacked[1].astype(jnp.float32) + bias_ref[...])
    total = total.astype(jnp.bfloat16).astype(jnp.float32)
    lanes = channels // LANES
    for block in range(lanes):
        held[block, 8:, :] = total[:, block * LANES : (block + 1) * LANES]
    half = columns // 2
    first = lax.broadcasted_iota(jnp.int32, (rows * half, LANES), 0) % half == 0
    for place in range(frames):
        for block in range(lanes):
            begin = place * count
            moved = held[block, pl.ds(begin + 7, rows * half, stride=2), :]
            even = held[block, pl.ds(begin + 8, rows * half, stride=2), :]
            odd = held[block, pl.ds(begin + 9, rows * half, stride=2), :]
            moved = jnp.where(first, 0.0, moved)
            for tap, plane in enumerate((moved, even, odd)):
                start = tap * channels + block * LANES
                out_ref[:, place, :, start : start + LANES] = plane.astype(jnp.bfloat16).reshape(
                    rows, half, LANES
                )


def from_row(step, start, columns, channels):
    return pl.BlockSpec((1, step, columns, channels), lambda r: (0, r + start // step, 0, 0))


def temporal(sequence, time_weight, time_bias, start, rows, step):
    _, _, columns, channels = sequence[0].shape
    frames = len(sequence) - 2
    half = columns // 2
    return pl.pallas_call(
        temporal_kernel,
        out_shape=jax.ShapeDtypeStruct((rows, frames, half, 3 * channels), jnp.bfloat16),
        grid=(rows // step,),
        in_specs=[from_row(step, start, columns, channels)] * len(sequence)
        + [
            pl.BlockSpec((3 * channels, channels), lambda r: (0, 0)),
            pl.BlockSpec((1, channels), lambda r: (0, 0)),
        ],
        out_specs=pl.BlockSpec((step, frames, half, 3 * channels), lambda r: (r, 0, 0, 0)),
        scratch_shapes=[pltpu.VMEM((channels // LANES, 8 + frames * step * columns, LANES), jnp.float32)],
        cost_estimate=pl.CostEstimate(
            flops=6 * frames * rows * columns * channels * channels,
            bytes_accessed=2 * (5 * frames + 2) * rows * columns * channels,
            transcendentals=0,
        ),
    )(*sequence, time_weight.reshape(3 * channels, channels), time_bias)


def strided_kernel(spans, parts, where_ref, upper_ref, bias_ref, *refs):
    planes_refs, refs = refs[:parts], refs[parts:]
    pieces, (out_ref, weight, total, sems) = refs[: len(spans)], refs[len(spans) :]
    step = pl.program_id(0)
    _, _, frames, half_cols, width = planes_refs[0].shape
    half_rows = sum(ref.shape[0] for ref in planes_refs)
    count = half_rows * frames * half_cols
    channels = width // 3
    _, units, unit, _ = weight.shape

    def load(place, piece, run, at):
        tap = where_ref[place, 0] + at
        lanes = pl.ds(pl.multiple_of(tap % 3 * channels, LANES), channels)
        target = weight.at[tap // 3, pl.ds(where_ref[place, 1], run), :, lanes]
        pltpu.make_async_copy(piece.at[at], target, sems.at[tap // 3]).start()

    def product(values, tap):
        pltpu.make_async_copy(weight.at[tap], weight.at[tap], sems.at[tap]).wait()
        return lax.dot_general(
            values.reshape(count, width),
            weight[tap].reshape(units * unit, width),
            (((1,), (1,)), ((), ())),
            preferred_element_type=jnp.float32,
        )

    @pl.when(step == 0)
    def _():
        for place, (piece, (taps, run)) in enumerate(zip(pieces, spans)):
            for at in range(taps):
                load(place, piece, run, at)
        values = jnp.concatenate([upper_ref[...]] + [ref[:, 0] for ref in planes_refs], axis=0)[:half_rows]
        total[...] = product(values, 0) + bias_ref[...]

    @pl.when(step == 1)
    def _():
        total[...] += product(jnp.concatenate([ref[:, 0] for ref in planes_refs], axis=0), 2)

    @pl.when(step == 2)
    def _():
        done = total[...] + product(jnp.concatenate([ref[:, 0] for ref in planes_refs], axis=0), 1)
        out_ref[...] = done.astype(jnp.bfloat16).reshape(out_ref.shape)


def strided(planes, upper, pieces, where, bias, chunk, chunks):
    _, frames, all_cols, width = planes[0].shape
    half_cols = all_cols // chunks
    outputs = bias.shape[0]
    half_rows = sum(part.shape[0] for part in planes) // 2
    count = half_rows * frames * half_cols
    unit = pieces[0].shape[2]
    block = (half_rows, frames, half_cols, outputs)
    anywhere = pl.BlockSpec(memory_space=pl.ANY)
    return pl.pallas_call(
        functools.partial(strided_kernel, tuple(piece.shape[:2] for piece in pieces), len(planes)),
        out_shape=jax.ShapeDtypeStruct(block, jnp.bfloat16),
        grid=(3,),
        in_specs=[
            pl.BlockSpec(memory_space=pltpu.SMEM),
            pl.BlockSpec((1, frames, half_cols, width), lambda a: (0, 0, chunk, 0)),
            pl.BlockSpec((1, outputs), lambda a: (0, 0)),
        ]
        + [
            pl.BlockSpec(
                (part.shape[0] // 2, 1, frames, half_cols, width), lambda a: (0, 1 - a // 2, 0, chunk, 0)
            )
            for part in planes
        ]
        + [anywhere] * len(pieces),
        out_specs=pl.BlockSpec(block, lambda a: (0, 0, 0, 0)),
        scratch_shapes=[
            pltpu.VMEM((3, outputs // unit, unit, width), jnp.bfloat16),
            pltpu.VMEM((count, outputs), jnp.float32),
            pltpu.SemaphoreType.DMA((3,)),
        ],
        cost_estimate=pl.CostEstimate(
            flops=6 * count * width * outputs,
            bytes_accessed=2 * (2 * count * width + 3 * width * outputs + count * outputs),
            transcendentals=0,
        ),
    )(
        where,
        upper,
        bias.reshape(1, outputs),
        *(part.reshape(-1, 2, frames, all_cols, width) for part in planes),
        *pieces,
    )


def attention_kernel(
    tokens_ref, gain_ref, bias_ref, wq_hbm, wk_hbm, wv_hbm, wo_hbm, out_ref,
    wq, wk, wv, wo, held, normed, query, key, value, scores, weights, sems,
):
    copies = []
    for place, (source, target) in enumerate(((wq_hbm, wq), (wk_hbm, wk), (wv_hbm, wv), (wo_hbm, wo))):
        copies.append(pltpu.make_async_copy(source, target, sems.at[place]))
        copies[-1].start()
    frames, pixels, width = out_ref.shape
    groups = pixels // 8
    rows = frames * 8
    sources, span, _, half_width = tokens_ref.shape
    share = half_width // (sources // 2)
    head_width = width // HEADS
    scale = head_width ** (-0.5)
    for group in range(groups):
        here = slice(group * 8, group * 8 + 8)
        low = [tokens_ref[2 * line, :, here, :] for line in range(sources // 2)]
        high = [tokens_ref[2 * line + 1, span - 1 - at, here, :] for line in range(sources // 2) for at in range(span)]
        low = jnp.concatenate([value.astype(jnp.float32).reshape(span * 8, half_width) for value in low], axis=0)
        high = jnp.concatenate([value.astype(jnp.float32) for value in high], axis=0)
        parts = []
        for line in range(sources // 2):
            parts += [low[:, line * share : (line + 1) * share], high[:, line * share : (line + 1) * share]]
        tokens = jnp.concatenate(parts, axis=1)
        held[group * rows : (group + 1) * rows, :] = tokens.astype(jnp.bfloat16)
        centred = tokens - jnp.mean(tokens, axis=-1, keepdims=True)
        spread = jnp.mean(centred * centred, axis=-1, keepdims=True)
        result = centred * lax.rsqrt(spread + 1e-05) * gain_ref[...]
        normed[group * rows : (group + 1) * rows, :] = result.astype(jnp.bfloat16)
    for place, (weight, target) in enumerate(((wq, query), (wk, key), (wv, value))):
        copies[place].wait()
        target[...] = jnp.dot(normed[...], weight[...], preferred_element_type=jnp.float32).astype(jnp.bfloat16)

    same = (
        lax.broadcasted_iota(jnp.int32, (rows, rows), 0) % 8
        == lax.broadcasted_iota(jnp.int32, (rows, rows), 1) % 8
    )
    windows = []
    for head in range(HEADS):
        low = head * head_width // LANES
        high = ((head + 1) * head_width - 1) // LANES + 1
        lane = lax.broadcasted_iota(jnp.int32, (rows, (high - low) * LANES), 1) + low * LANES
        mine = (lane >= head * head_width) & (lane < (head + 1) * head_width)
        windows.append((low, high, mine))

    for group in range(groups):
        here = slice(group * rows, (group + 1) * rows)
        for head, (low, high, mine) in enumerate(windows):
            window = slice(low * LANES, high * LANES)
            queries = jnp.where(mine, query[here, window], jnp.zeros(mine.shape, jnp.bfloat16))
            scores[head] = lax.dot_general(
                queries, key[here, window], (((1,), (1,)), ((), ())), preferred_element_type=jnp.float32
            )

        @pl.loop(0, HEADS // 4)
        def _(quarter):
            part = pl.ds(quarter * 4, 4)
            some = jnp.where(same[None], scores[part] * scale, MASKED)
            powers = jnp.exp(some - jnp.max(some, axis=-1, keepdims=True))
            share_of = 1.0 / jnp.sum(powers, axis=-1, keepdims=True)
            weights[part] = (powers * share_of).astype(jnp.bfloat16)

        sums = [None] * (width // LANES)
        for head, (low, high, mine) in enumerate(windows):
            window = slice(low * LANES, high * LANES)
            values = jnp.where(mine, value[here, window], jnp.zeros(mine.shape, jnp.bfloat16))
            part = jnp.dot(weights[head], values, preferred_element_type=jnp.float32)
            for block in range(low, high):
                piece = part[:, (block - low) * LANES : (block - low + 1) * LANES]
                sums[block] = piece if sums[block] is None else sums[block] + piece
        for block, total in enumerate(sums):
            normed[here, block * LANES : (block + 1) * LANES] = total.astype(jnp.bfloat16)

    copies[3].wait()
    output = jnp.dot(normed[...], wo[...], preferred_element_type=jnp.float32)
    output = output + bias_ref[...] + held[...].astype(jnp.float32)
    for group in range(groups):
        piece = output[group * rows : (group + 1) * rows].reshape(frames, 8, width)
        out_ref[:, group * 8 : group * 8 + 8, :] = piece.astype(jnp.bfloat16)


def attention(tokens, norm_gain, out_bias, w_query, w_key, w_value, w_out):
    sources, span, pixels, half_width = tokens.shape
    frames, width = sources * span // 2, 2 * half_width
    count = frames * pixels
    weight = pltpu.VMEM((width, width), jnp.bfloat16)
    rows = pltpu.VMEM((count, width), jnp.bfloat16)
    anywhere = pl.BlockSpec(memory_space=pl.ANY)
    inside = pl.BlockSpec(memory_space=pltpu.VMEM)
    return pl.pallas_call(
        attention_kernel,
        out_shape=jax.ShapeDtypeStruct((frames, pixels, width), jnp.bfloat16),
        in_specs=[inside, inside, inside, anywhere, anywhere, anywhere, anywhere],
        out_specs=inside,
        scratch_shapes=[weight] * 4
        + [rows] * 5
        + [
            pltpu.VMEM((HEADS, frames * 8, frames * 8), jnp.float32),
            pltpu.VMEM((HEADS, frames * 8, frames * 8), jnp.bfloat16),
            pltpu.SemaphoreType.DMA((4,)),
        ],
        cost_estimate=pl.CostEstimate(
            flops=8 * count * width * width,
            bytes_accessed=8 * width * width + 4 * count * width,
            transcendentals=count * HEADS * frames * 8,
        ),
    )(
        tokens, norm_gain.reshape(1, width), out_bias.reshape(1, width), w_query, w_key, w_value, w_out
    )


def on_device(
    features,
    time_weight,
    time_bias,
    down_weight,
    down_bias,
    norm_gain,
    w_query,
    w_key,
    w_value,
    w_out,
    out_bias,
):
    frames_here, rows_here, columns, channels = features.shape
    groups = lax.axis_size("frame")
    lines = groups // 2
    frame, row = lax.axis_index("frame"), lax.axis_index("row")
    side = frame % 2

    everyone = range(groups)
    swapped = [(at, at ^ 1) for at in everyone]
    outward = [(at, at + (2 if at % 2 else -2)) for at in everyone]
    inward = [(at, at + (-2 if at % 2 else 2)) for at in everyone]
    inside = lambda pairs: [(source, target) for source, target in pairs if 0 <= target < groups]
    half = rows_here // 2
    starts = (half, 0)

    def own_frame(at, start):
        place = jnp.where(side == 0, at, frames_here - 1 - at)
        return lax.dynamic_slice(features, (place, start, 0, 0), (1, half, columns, channels))

    def moved_along(value, pairs):
        return lax.ppermute(value, "frame", pairs)

    own = [[own_frame(at, start) for at in range(frames_here)] for start in starts]
    outer = [moved_along(value[0], swapped) for value in own]
    last = [moved_along(value[0], inside(outward)) for value in own]
    first = [moved_along(value, inside(inward)) for value in outer]
    inner = [[moved_along(each, swapped) for each in value[1:]] for value in own]
    sequences = [
        [first[part]] + own[part] + inner[part][::-1] + [outer[part], last[part]] for part in range(len(starts))
    ]

    pieces, where = strided_weights(down_weight, frame, row, channels)

    taps = jnp.where(side == 0, time_weight, time_weight[::-1])
    bias_row = time_bias.reshape(1, channels)
    lower_planes = temporal(sequences[0], taps, bias_row, 0, half, 2)
    upper = passed_along(lower_planes[-1:], "row", 1)
    upper_planes = temporal(sequences[1], taps, bias_row, 0, half, 2)
    planes = [upper_planes, lower_planes]
    shares = down_bias.reshape(lines, 2, down_bias.shape[0] // groups)
    bias = lax.dynamic_index_in_dim(shares, side, axis=1, keepdims=False).reshape(-1)

    half_rows, half_cols = rows_here // 2, columns // 2
    pixels_here = half_rows * half_cols // groups
    chunks = 2 if groups == half_rows and pixels_here % 16 == 0 else 1
    moved, results = [], []
    part = pixels_here // chunks
    for at in range(chunks):
        coarse = strided(planes, upper, pieces, where, bias, at, chunks)
        half_width = coarse.shape[-1]
        tokens = coarse
        if groups != half_rows:
            tokens = tokens.transpose(1, 0, 2, 3).reshape(2 * frames_here, groups, part, half_width)
            tokens = tokens.transpose(1, 0, 2, 3)
        moved.append(lax.all_to_all(tokens, "frame", split_axis=0, concat_axis=0, tiled=True))
    for tokens in moved:
        result = attention(tokens, norm_gain, out_bias, w_query, w_key, w_value, w_out)
        result = result.reshape(groups, frames_here, part, 2 * half_width)
        results.append(lax.all_to_all(result, "frame", split_axis=0, concat_axis=0, tiled=True))
    returned = jnp.concatenate(results, axis=2).transpose(1, 0, 2, 3)
    return returned.reshape(frames_here, half_rows, half_cols, 2 * half_width)


def strided_weights(down_weight, frame, row, channels):
    groups, row_devices = lax.axis_size("frame"), lax.axis_size("row")
    lines = groups // 2
    share = down_weight.shape[3]
    line = frame // 2
    shard = down_weight.transpose(0, 1, 3, 2).reshape(9, share, channels)
    unit = share // 2
    if unit % 16 or lines & (lines - 1) or row_devices % 4:
        members = [[2 * at + side for at in range(lines)] for side in range(2)]
        gathered = lax.all_gather(shard, "frame", axis=1, tiled=True, axis_index_groups=members)
        return [gathered[:, None]], jnp.zeros((1, 2), jnp.int32)
    core, plane = row % 2, row // 2 % 2
    shard = shard.reshape(9, 2, unit, channels)
    pieces = [shard]
    mine = lax.dynamic_slice(shard, (4 * plane, core, 0, 0), (5, 1, unit, channels))
    rows = range(row_devices)

    def along(value, pairs):
        steps = [(2 * source + at, 2 * target + at) for source, target in pairs for at in range(2)]
        return lax.ppermute(value, "frame", steps)

    nears = {}
    for distance in range(1, lines):
        if lines == 4 and distance == 3:
            middle = along(mine, [(1, 2), (2, 1)])
            near = middle + along(nears[2], [(1, 0), (2, 3)])
        else:
            near = along(mine, [(at, at ^ distance) for at in range(lines)])
        nears[distance] = near
        sent = lax.dynamic_slice_in_dim(near, plane, 4, axis=0)
        far = lax.ppermute(sent, "row", [(at, at ^ 2) for at in rows])
        pieces += [near, far]
        for value in (near, far):
            pieces.append(lax.ppermute(value, "row", [(at, at ^ 1) for at in rows]))

    def places(line, plane, core):
        found = [(0, 2 * line)]
        for distance in range(1, lines):
            for half in (core, 1 - core):
                at = 2 * (line ^ distance) + half
                found += [(4 * plane, at), (5 - 5 * plane, at)]
        return found

    table = [places(at // 4, at // 2 % 2, at % 2) for at in range(4 * lines)]
    table = jnp.asarray(np.array(table, np.int32))
    where = lax.dynamic_index_in_dim(table, 4 * line + 2 * plane + core, 0, keepdims=False)
    return pieces, where


def solution(mesh):
    return jax.shard_map(
        on_device,
        mesh=mesh,
        in_specs=(
            P("frame", "row", None, None),
            P(),
            P(),
            P(None, None, None, "frame"),
            P(),
            P(),
            P(),
            P(),
            P(),
            P(),
            P(),
        ),
        out_specs=P("frame", "row", None, None),
        check_vma=False,
    )
```
